256 devices in a mesh: space: 32 (over z, x), tm: 8 (over y, core).
Axes of the slice: x: 4, y: 4, z: 8, core: 2. Of those that a mesh axis runs over, the one named last changes fastest.
Arguments:
- iterate: float32 [8, 240, 23040], P(None, 'tm', 'space'), may hold values from -6 to 6
- residual: float32 [8, 240, 23040], P(None, 'tm', 'space'), may hold values from -24 to 24
- direction: float32 [8, 240, 23040], P(None, 'tm', 'space'), may hold values from -24 to 24
- diffusivity: float32 [23040], P('space'), may hold values from 0.1 to 0.34
- temporal_factor: float32 [240, 240], replicated, may hold values from 0 to 4
- block_tile: int32 [8, 256], P('tm', 'space'), may hold values from -1 to 479, as said below
- footprints: bfloat16 [8, 256, 64, 1440], P('tm', 'space'), may hold values from -0.15625 to 0.15625
- obs_weight: float32 [8, 32, 64], P('tm', 'space'), may hold values from 0.3 to 3
Outputs:
- iterate_next: float32 [8, 240, 23040], P(None, 'tm', 'space')
- residual_next: float32 [8, 240, 23040], P(None, 'tm', 'space')
- direction_next: float32 [8, 240, 23040], P(None, 'tm', 'space')
The draws below stay inside these ranges and needn't reach their ends.
Inputs may be any that keep to these rules, and one draw needn't show every extreme that they name: `block_tile`: entry -1 marks a padding slot. Tile g belongs to index g // 15 of space. The valid entries of one device name distinct tiles, at most 2 of them of one owner; in each row of tm one owner is named exactly 2 times by every device.
All inputs are finite; a program needn't handle non-finite values.
Results may differ from the reference program's by a relative error of at most 0.017.
Values may be sent and summed in bfloat16 or wider, within the bound.
No kernel may reach another device: no remote copies, remote signals or barrier semaphores. Data moves between devices by JAX's collectives and lax.ppermute only.
A program may use at most 128 MiB of HBM per device.

```python
import math
import jax
import jax.numpy as jnp
from jax import lax

S = 8
NT = 240
LON = 720
TC = 48
NB = 8
SB = 64
BATCH_DEV = 1
DIFF = 2
TW = 30
NLAT = 32
CELLS = 23040
TILES_DEV = 15
TILES = 480
BLOCKS_DEV = 8
CAP = 2
N_SPACE = 32
N_TM = 8


def scaled_field(key, marker):
    folded = jax.random.fold_in(key, marker)
    first_key = jax.random.fold_in(folded, 0)
    layout = (S, NT, CELLS)
    latitude = (jnp.arange(CELLS) // LON).astype(jnp.float32)
    growth = 4.0 ** (latitude / max(NLAT - 1, 1))
    return jnp.clip(jax.random.normal(first_key, layout, jnp.float32), -6.0, 6.0) * growth


def draw_residual(key, part):
    return scaled_field(key, 11)


def draw_direction(key, part):
    return scaled_field(key, 23)


def draw_temporal_factor(key, part):
    steps_index = jnp.arange(NT)
    distance = jnp.abs(steps_index[:, None] - steps_index[None, :]).astype(jnp.float32)
    length_scale = NT / 4.0
    lower_end, upper_end = (0.5, 1.5)
    weights = jax.random.uniform(jax.random.fold_in(key, 37), (NT, NT), jnp.float32, lower_end, upper_end)
    return (2.0 * jnp.eye(NT, dtype=jnp.float32) + jnp.exp(-distance / length_scale) * weights) / math.sqrt(length_scale)


def draw_block_tile(key, part):
    hot_key, rest_key = jax.random.split(jax.random.fold_in(key, 53))
    popular = jax.random.randint(hot_key, (N_TM,), 0, N_SPACE)
    others_count = (N_SPACE - 1) * CAP

    def device_list(device_key, favored):
        pick_key, offset_key, padding_key, order_key = jax.random.split(device_key, 4)
        counter = jnp.arange(others_count)
        other_owner = (favored + 1 + counter // CAP) % N_SPACE
        other_rank = counter % CAP
        chosen = jax.random.permutation(pick_key, others_count)[:BLOCKS_DEV - CAP]
        owners = jnp.concatenate([jnp.full((CAP,), favored, jnp.int32), other_owner[chosen].astype(jnp.int32)])
        ranking = jnp.concatenate([jnp.arange(CAP, dtype=jnp.int32), other_rank[chosen].astype(jnp.int32)])
        offsets = jax.random.randint(offset_key, (N_SPACE,), 0, TILES_DEV)
        local_tile = (offsets[owners] + ranking) % TILES_DEV
        padded = (jax.random.randint(padding_key, (BLOCKS_DEV,), 0, 5) == 0) & (jnp.arange(BLOCKS_DEV) >= CAP)
        entries = jnp.where(padded, -1, owners * TILES_DEV + local_tile)
        return entries[jax.random.permutation(order_key, BLOCKS_DEV)]
    device_keys = jax.random.split(rest_key, N_TM * N_SPACE)
    device_keys = device_keys.reshape((N_TM, N_SPACE) + device_keys.shape[1:])
    per_device = jax.vmap(jax.vmap(device_list, in_axes=(0, None)), in_axes=(0, 0))(device_keys, popular)
    return per_device.reshape(N_TM, N_SPACE * BLOCKS_DEV).astype(jnp.int32)


def block_levels(stream_key, extent, cuts, low, largest):
    loudness = 1.0
    for position, blocks in cuts:
        heights = jax.random.uniform(jax.random.fold_in(jax.random.fold_in(stream_key, 6), position), (blocks,), jnp.float32, low / len(cuts), largest / len(cuts))
        loudness = loudness * jnp.repeat(jnp.exp(heights), extent[position] // blocks).reshape((-1,) + (1,) * (len(extent) - 1 - position))
    return loudness


def gaussian(rng, extent, scale, limit, cuts=(), held_as=jnp.bfloat16):
    level = block_levels(rng, extent, cuts, -0.22, 0.18) if cuts else 1.0
    values = jax.random.normal(rng, extent, jnp.float32) * scale * level
    return jnp.minimum(jnp.maximum(values, -limit), limit).astype(held_as)


def setup_inputs(seed: int = 0) -> dict:
    keys = jax.random.split(jax.random.key(seed), 9)
    iterate = gaussian(keys[0], (S, NT, CELLS), 1.0, 6.0, ((1, 8), (2, 32)), jnp.float32)
    residual = draw_residual(jax.random.fold_in(keys[8], 71), 0)
    direction = draw_direction(jax.random.fold_in(keys[8], 71), 0)
    diffusivity = jnp.clip(jnp.exp(math.log(0.34) - 1.2237754 * jax.random.uniform(keys[3], (CELLS,), jnp.float32) ** block_levels(keys[3], (CELLS,), ((0, 32),), -0.2, 0.2)), 0.1, 0.34)
    temporal_factor = draw_temporal_factor(jax.random.fold_in(keys[8], 71), 0)
    block_tile = draw_block_tile(jax.random.fold_in(keys[8], 71), 0)
    footprints = gaussian(keys[6], (N_TM, N_SPACE * BLOCKS_DEV, SB, TW * TC), (TW * TC) ** -0.5, 0.15625, ((0, 8), (1, 32)))
    obs_weight = jnp.clip(jnp.exp(math.log(3.0) - 2.3025851 * jax.random.uniform(keys[7], (N_TM, N_SPACE * BATCH_DEV, SB), jnp.float32) ** block_levels(keys[7], (N_TM, N_SPACE * BATCH_DEV, SB), ((0, 8), (1, 32)), -0.2, 0.2)), 0.3, 3.0)
    return {"iterate": iterate, "residual": residual, "direction": direction, "diffusivity": diffusivity, "temporal_factor": temporal_factor, "block_tile": block_tile, "footprints": footprints, "obs_weight": obs_weight}


def diffuse(field, diffusivity):
    conduct = diffusivity.reshape(NLAT, LON)
    samples = field.shape[0]
    for sweep_index in range(DIFF):
        scaled_grid = field.reshape(samples, NT, NLAT, LON) * conduct
        padded = jnp.pad(scaled_grid, ((0, 0), (0, 0), (1, 1), (0, 0)))
        laplace = padded[:, :, :-2, :] + padded[:, :, 2:, :] + jnp.roll(scaled_grid, 1, 3) + jnp.roll(scaled_grid, -1, 3) - 4.0 * scaled_grid
        field = field + (conduct * laplace).reshape(samples, NT, CELLS)
    return field


def observe_adjoint(flux16, block_tile, footprints, obs_weight):
    samples = flux16.shape[0]
    windows_out = []
    for window_index in range(N_TM):
        window_flux = flux16[:, window_index * TW:(window_index + 1) * TW, :].reshape(samples, TW, TILES, TC)
        tile_table = jnp.transpose(window_flux, (2, 0, 1, 3)).reshape(TILES, samples, TW * TC)
        entries = block_tile[window_index]
        present = entries >= 0
        blocks = jnp.where(present[:, None, None], tile_table[jnp.maximum(entries, 0)], jnp.zeros((), jnp.bfloat16))
        footprint = footprints[window_index].astype(jnp.float32)
        slot_obs = jnp.einsum('bmx,bkx->bkm', footprint, blocks.astype(jnp.float32), precision=lax.Precision.HIGHEST)
        batch_obs = jnp.sum(slot_obs.reshape(-1, NB, samples, SB), axis=1)
        weighted = lax.optimization_barrier((obs_weight[window_index][:, None, :] * batch_obs).astype(jnp.bfloat16))
        grouped = footprint.reshape(-1, NB, SB, TW * TC)
        gradient = jnp.einsum('anmx,akm->ankx', grouped, weighted.astype(jnp.float32), precision=lax.Precision.HIGHEST)
        gradient = gradient.reshape(-1, samples, TW * TC)
        gradient = jnp.where(present[:, None, None], gradient, jnp.zeros((), jnp.float32))
        gradient = lax.optimization_barrier(gradient.astype(jnp.bfloat16)).astype(jnp.float32)
        destination = jnp.where(present, entries, TILES).astype(jnp.int32)
        summed = jax.ops.segment_sum(gradient, destination, num_segments=TILES + 1)[:TILES]
        summed = summed.reshape(TILES, samples, TW, TC).transpose(1, 2, 0, 3).reshape(samples, TW, CELLS)
        windows_out.append(summed)
    return jnp.concatenate(windows_out, axis=1)


def reference(iterate, residual, direction, diffusivity, temporal_factor, block_tile, footprints, obs_weight):
    mixed = jnp.einsum('tu,kuc->ktc', temporal_factor, direction, precision=lax.Precision.HIGHEST)
    spread = diffuse(mixed, diffusivity)
    flux16 = spread.astype(jnp.bfloat16)
    pulled = observe_adjoint(flux16, block_tile, footprints, obs_weight)
    back = diffuse(pulled, diffusivity)
    image = direction + jnp.einsum('ut,kuc->ktc', temporal_factor, back, precision=lax.Precision.HIGHEST)
    old_norm = jnp.sum(residual * residual, axis=(1, 2))
    curvature = jnp.sum(direction * image, axis=(1, 2))
    step_size = old_norm / curvature
    residual_next = residual - step_size[:, None, None] * image
    iterate_next = iterate + step_size[:, None, None] * direction
    new_norm = jnp.sum(residual_next * residual_next, axis=(1, 2))
    direction_next = residual_next + (new_norm / old_norm)[:, None, None] * direction
    return (iterate_next, residual_next, direction_next)
```

```python
import jax
import jax.numpy as jnp
from jax import lax
from jax.experimental import pallas as pl
from jax.experimental.pallas import tpu as pltpu
from jax.sharding import PartitionSpec as P

LON = 720
TC = 48
NB = 8
DIFF = 2
LANES = 128
WIDE = 768
PIECES = WIDE // LANES
ROWS = 32
TW = 30
TWP = 32
NW = 8
COLS = LON // TC
BLANK = COLS * ROWS
TAIL = LON - (PIECES - 1) * LANES
IDX = 82
F32 = jnp.float32
BF16 = jnp.bfloat16


def call(body, outs, scratch=(), scalars=0):
    def run(*args):
        specs = [smem() if i < scalars else vmem() for i in range(len(args))]
        return pl.pallas_call(
            body,
            out_shape=outs,
            in_specs=specs,
            scratch_shapes=list(scratch),
            compiler_params=pltpu.CompilerParams(vmem_limit_bytes=40 * 1024 * 1024),
        )(*args)

    return run


def vmem():
    return pl.BlockSpec(memory_space=pltpu.VMEM)


def smem():
    return pl.BlockSpec(memory_space=pltpu.SMEM)


def lanes_of(shape):
    return lax.broadcasted_iota(jnp.int32, shape, len(shape) - 1)


def turn(value, shift):
    shift = shift % value.shape[-1]
    return value if shift == 0 else pltpu.roll(value, shift, value.ndim - 1)


def span(start, source, length=TC):
    parts = []
    done = 0
    while done < length:
        a, b = (source + done) // LANES, (start + done) // LANES
        take = min(length - done, (a + 1) * LANES - source - done, (b + 1) * LANES - start - done)
        low = start + done - b * LANES
        parts.append((a, b, low, low + take, (start - source) % LANES))
        done += take
    return parts


def chain(parts, lane, below=None):
    parts = sorted(parts, key=lambda part: part[0])
    result = parts[-1][2]
    for low, high, value in reversed(parts[:-1]):
        result = jnp.where(lane < high, value, result)
    return result


def prepare_body(tile_ref, d_ref, factor_ref, out_ref, hi_ref, lo_ref, z_ref, wide_ref, deep_ref, tail_ref):
    tail_ref[:, 0:TAIL] = d_ref[:, (PIECES - 1) * LANES : LON]
    lane = lanes_of((240, LANES))
    for q in range(PIECES - 1):
        z_ref[q, 0:240, :] = d_ref[:, q * LANES : (q + 1) * LANES]
        z_ref[q, 240:256, :] = jnp.zeros((16, LANES), F32)
    tail = tail_ref[...]
    first = d_ref[:, 0:LANES]
    last = jnp.where(
        lane < TAIL,
        tail,
        jnp.where(lane < TAIL + 2, turn(first, TAIL), jnp.where(lane >= LANES - 2, turn(tail, TC), 0.0)),
    )
    z_ref[PIECES - 1, 0:240, :] = last
    line = lanes_of((8, LANES))
    codes = jnp.zeros((8, LANES), F32)
    for j in range(NB):
        tile = tile_ref[0, j]
        there = tile >= 0
        safe = jnp.maximum(tile, 0)
        row = (safe * 4370) >> 16
        col = safe - row * COLS
        row = jnp.where(there, row, 0).astype(F32)
        col = jnp.where(there, col, COLS).astype(F32)
        codes = jnp.where(line == IDX + j, row, codes)
        codes = jnp.where(line == IDX + NB + j, col, codes)
    z_ref[PIECES - 1, 240:248, :] = codes
    z_ref[PIECES - 1, 248:256, :] = jnp.zeros((8, LANES), F32)
    for q in range(PIECES):
        for k in range(8):
            out_ref[k, :, q * LANES : (q + 1) * LANES] = z_ref.at[q][pl.ds(k, TWP, stride=8), :].astype(BF16)
    wide_ref[:, LANES:] = jnp.zeros((240, LANES), F32)
    wide_ref[:, 0:240] = factor_ref[...]
    factor = wide_ref[...]
    column = lanes_of((240, 256))
    padded = jnp.zeros((240, 256), F32)
    for w in range(NW):
        here = ((column >> 5) == w) & ((column & 31) < TW)
        padded = jnp.where(here, turn(factor, 2 * w), padded)
    wide_ref[...] = padded
    deep_ref[...] = jnp.zeros((256, 256), F32)
    for w in range(NW):
        deep_ref[TWP * w : TWP * w + TW, :] = wide_ref[TW * w : TW * w + TW, :]
    rows = lax.broadcasted_iota(jnp.int32, (256, 256), 0)
    column = lanes_of((256, 256))
    codes_here = ((column & 31) == TW) & ((rows >> 5) == (column >> 5)) & ((rows & 31) < TW)
    full = jnp.where(codes_here, 1.0, deep_ref[...])
    hi = full.astype(BF16)
    hi_ref[...] = hi
    lo_ref[...] = (full - hi.astype(F32)).astype(BF16)


def mix_body(x_ref, hi_ref, lo_ref, conduct_ref, out_ref, z_ref, k_ref, row_ref):
    x = x_ref[...]
    mixed = jnp.dot(hi_ref[...], x, preferred_element_type=F32) + jnp.dot(
        lo_ref[...], x, preferred_element_type=F32
    )
    for w in range(NW):
        for q in range(PIECES):
            z_ref[pl.ds(w * 8 + q, TWP, stride=64), :] = mixed[TWP * w : TWP * (w + 1), q * LANES : (q + 1) * LANES]
    lane = lanes_of((1, LANES))
    row_ref[...] = jnp.zeros((8, LANES), F32)
    row_ref[0:1, 0:TAIL] = conduct_ref[0:1, (PIECES - 1) * LANES : LON]
    tail = row_ref[0:1, :]
    first = conduct_ref[0:1, 0:LANES]
    last = jnp.where(
        lane < TAIL,
        tail,
        jnp.where(lane < TAIL + 2, turn(first, TAIL), jnp.where(lane >= LANES - 2, turn(tail, TC), 0.0)),
    )
    k_ref[...] = jnp.zeros((16, LANES), F32)
    for q in range(PIECES):
        part = last if q == PIECES - 1 else conduct_ref[0:1, q * LANES : (q + 1) * LANES]
        hi = part.astype(BF16).astype(F32)
        k_ref[q : q + 1, :] = hi
        k_ref[PIECES + q : PIECES + q + 1, :] = part - hi
    m = lax.axis_index("tm")
    for e in range(2):
        part = k_ref[pl.ds(2 * m + e, 1), :]
        z_ref[pl.ds(6 + e, 256, stride=8), :] = jnp.broadcast_to(part, (256, LANES))
    out_ref[...] = z_ref[...].astype(BF16)


def diffuse_rows(w_ref, u_ref, k_ref):
    u_ref[0] = jnp.zeros((8, WIDE), F32)
    u_ref[ROWS + 1] = jnp.zeros((8, WIDE), F32)
    for step in range(DIFF):
        for s in range(ROWS):
            u_ref[s + 1] = w_ref[s] * k_ref[s : s + 1, :]
        for s in range(ROWS):
            u = u_ref[s + 1]
            laplace = u_ref[s] + u_ref[s + 2] + turn(u, 1) + turn(u, -1) - 4.0 * u
            w_ref[s] = w_ref[s] + k_ref[s : s + 1, :] * laplace


def spread_body(slot_ref, x_ref, out_ref, kept_ref, z_ref, w_ref, u_ref, table_ref):
    z_ref[...] = x_ref[...].astype(F32)
    for q in range(PIECES):
        hi, lo = q, PIECES + q
        kept_ref[:, q * LANES : (q + 1) * LANES] = (
            z_ref[pl.ds((hi // 2) * 8 + 6 + hi % 2, ROWS, stride=64), :]
            + z_ref[pl.ds((lo // 2) * 8 + 6 + lo % 2, ROWS, stride=64), :]
        )
        for s in range(ROWS):
            w_ref[s, :, q * LANES : (q + 1) * LANES] = z_ref[pl.ds(s * 64 + q, 8, stride=8), :]
    diffuse_rows(w_ref, u_ref, kept_ref)
    lane = lanes_of((8, LANES))
    for s in range(ROWS):
        for c in range(COLS):
            parts = [
                (low, high, turn(w_ref[s, :, a * LANES : (a + 1) * LANES], rotation))
                for a, _, low, high, rotation in span(0, c * TC)
            ]
            table_ref[c * ROWS + s] = chain(parts, lane)
    table_ref[BLANK] = jnp.zeros((8, LANES), F32)

    def reader(s, carry):
        runs = [[], [], []]
        for j in range(NB):
            tile = table_ref[slot_ref[s * NB + j]]
            for _, b, low, high, rotation in span(j * TC, 0):
                runs[b].append((low, high, turn(tile, rotation)))
        for b in range(3):
            out_ref[s, :, b * LANES : (b + 1) * LANES] = chain(runs[b], lane).astype(BF16)
        return carry

    lax.fori_loop(0, ROWS, reader, 0)


def observe_body(x_ref, f_ref, weight_ref, out_ref, x2_ref, g_ref):
    lane = lanes_of((8, LANES))
    runs = {}
    for tau in range(TW):
        value = x_ref[tau].astype(F32)
        for j in range(NB):
            for a, b, low, high, rotation in span(tau * TC, j * TC):
                piece = turn(value[:, a * LANES : (a + 1) * LANES], rotation)
                runs.setdefault((j, b), []).append((low, high, piece))
        for key in [key for key in runs if (key[1] + 1) * LANES <= (tau + 1) * TC or tau == TW - 1]:
            j, b = key
            x2_ref[j, :, b * LANES : (b + 1) * LANES] = chain(runs.pop(key), lane)
    total = jnp.zeros((8, 64), F32)
    for j in range(NB):
        total = total + lax.dot_general(
            x2_ref[j, :, 0 : TW * TC].astype(BF16),
            f_ref[j],
            (((1,), (1,)), ((), ())),
            preferred_element_type=F32,
        )
    weighted = (weight_ref[...] * total).astype(BF16)
    for j in range(NB):
        g_ref[j, :, 0 : TW * TC] = jnp.dot(weighted, f_ref[j], preferred_element_type=F32)
    for tau in range(TW):
        runs = [[], [], []]
        for j in range(NB):
            for a, b, low, high, rotation in span(j * TC, tau * TC):
                runs[b].append((low, high, turn(g_ref[j, :, a * LANES : (a + 1) * LANES], rotation)))
        for b in range(3):
            out_ref[tau, :, b * LANES : (b + 1) * LANES] = chain(runs[b], lane).astype(BF16)
    out_ref[TW:TWP] = jnp.zeros((TWP - TW, 8, NB * TC), BF16)


def collect_body(slot_ref, x_ref, k_ref, out_ref, z_ref, w_ref, u_ref, table_ref):
    lane = lanes_of((8, LANES))
    table_ref[...] = jnp.zeros(table_ref.shape, F32)

    def reader(s, carry):
        value = x_ref[s].astype(F32)
        for j in range(NB):
            parts = [
                (low, high, turn(value[:, a * LANES : (a + 1) * LANES], rotation))
                for a, _, low, high, rotation in span(0, j * TC)
            ]
            g = slot_ref[s * NB + j]
            table_ref[g] = table_ref[g] + chain(parts, lane)
        return carry

    lax.fori_loop(0, ROWS, reader, 0)
    for s in range(ROWS):
        runs = [[] for _ in range(PIECES)]
        for c in range(COLS):
            tile = table_ref[c * ROWS + s]
            for _, b, low, high, rotation in span(c * TC, 0):
                runs[b].append((low, high, turn(tile, rotation)))
        runs[-1].append((TAIL, TAIL + 2, turn(table_ref[s], TAIL)))
        runs[-1].append((TAIL + 2, LANES - 2, jnp.zeros((8, LANES), F32)))
        runs[-1].append((LANES - 2, LANES, turn(table_ref[(COLS - 1) * ROWS + s], TAIL)))
        for b in range(PIECES):
            w_ref[s, :, b * LANES : (b + 1) * LANES] = chain(runs[b], lane)
    diffuse_rows(w_ref, u_ref, k_ref)
    for s in range(ROWS):
        for q in range(PIECES):
            z_ref[pl.ds(s * 64 + q, 8, stride=8), :] = w_ref[s, :, q * LANES : (q + 1) * LANES]
        for q in range(PIECES, 8):
            z_ref[pl.ds(s * 64 + q, 8, stride=8), :] = jnp.zeros((8, LANES), F32)
    out_ref[...] = z_ref[...].astype(BF16)


def unmix_body(x_ref, hi_ref, lo_ref, out_ref, z_ref, w_ref):
    z_ref[...] = x_ref[...].astype(F32)
    for w in range(NW):
        for q in range(PIECES):
            w_ref[TWP * w : TWP * (w + 1), q * LANES : (q + 1) * LANES] = z_ref[
                pl.ds(w * 8 + q, TWP, stride=64), :
            ].astype(BF16)
    x = w_ref[...]
    down = (((0,), (0,)), ((), ()))
    mixed = lax.dot_general(hi_ref[...], x, down, preferred_element_type=F32) + lax.dot_general(
        lo_ref[...], x, down, preferred_element_type=F32
    )
    out_ref[...] = mixed.astype(BF16)


def image_body(x_ref, d_ref, r_ref, image_ref, sums_ref, z_ref):
    for q in range(PIECES):
        z_ref[q] = x_ref[:, q * LANES : (q + 1) * LANES].astype(F32)
    totals = [jnp.zeros((8, 1), F32) for _ in range(4)]
    for q in range(PIECES):
        width = TAIL if q == PIECES - 1 else LANES
        at = pl.ds(q * LANES, width)
        sums = [jnp.zeros((8, width), F32) for _ in range(4)]
        for t in range(TW):
            d = d_ref[t, :, at]
            r = r_ref[t, :, at]
            image = d + z_ref.at[q][pl.ds(t, 8, stride=TWP), :][:, 0:width]
            image_ref[t, :, at] = image
            for i, (left, right) in enumerate(((r, r), (d, image), (r, image), (image, image))):
                sums[i] = sums[i] + left * right
        for i in range(4):
            totals[i] = totals[i] + jnp.sum(sums[i], axis=1, keepdims=True)
    lane = lanes_of((8, LANES))
    k = lax.broadcasted_iota(jnp.int32, (8, LANES), 0)
    spread = jnp.zeros((8, LANES), F32)
    for i in range(4):
        spread = jnp.where(lane == k * 4 + i, totals[i], spread)
    line = jnp.sum(spread, axis=0, keepdims=True)
    sums_ref[...] = jnp.broadcast_to(line, sums_ref.shape)


def update_body(sums_ref, it_ref, r_ref, d_ref, image_ref, it_out, r_out, d_out):
    line = jnp.sum(sums_ref[...], axis=0, keepdims=True)
    lane = lanes_of((8, LANES))
    k = lax.broadcasted_iota(jnp.int32, (8, LANES), 0)
    rr, dq, rq, qq = [
        jnp.sum(jnp.where(lane == k * 4 + i, line, 0.0), axis=1, keepdims=True) for i in range(4)
    ]
    step = rr / dq
    norm = jnp.maximum(rr + step * (step * qq - 2.0 * rq), 0.0)
    ratio = norm / rr
    for t in range(TW):
        d = d_ref[t]
        after = r_ref[t] - step * image_ref[t]
        it_out[t] = it_ref[t] + step * d
        r_out[t] = after
        d_out[t] = after + ratio * d


def shape(dims, dtype):
    return jax.ShapeDtypeStruct(dims, dtype)


def local(
    iterate, residual, direction, diffusivity, temporal_factor, block_tile, footprints, obs_weight
):
    both = ("space", "tm")
    iterate, residual, direction = [
        jnp.transpose(value, (1, 0, 2)) for value in (iterate, residual, direction)
    ]
    grid = (ROWS, 8, WIDE)
    with jax.named_scope("prepare"):
        message, hi, lo = call(
            prepare_body,
            (shape((8, TWP, WIDE), BF16), shape((256, 256), BF16), shape((256, 256), BF16)),
            [
                pltpu.VMEM((PIECES, 256, LANES), F32),
                pltpu.VMEM((240, 256), F32),
                pltpu.VMEM((256, 256), F32),
                pltpu.VMEM((240, LANES), F32),
            ],
            1,
        )(block_tile, direction.reshape(240, LON), temporal_factor)
        message = lax.all_to_all(message, "tm", 0, 0, tiled=True)
    with jax.named_scope("mix"):
        message = call(
            mix_body,
            shape((2048, LANES), BF16),
            [pltpu.VMEM((2048, LANES), F32), pltpu.VMEM((16, LANES), F32), pltpu.VMEM((8, LANES), F32)],
        )(message.reshape(256, WIDE), hi, lo, diffusivity.reshape(1, LON))
        message = lax.all_to_all(message.reshape(256, 8, LANES), both, 0, 0, tiled=True)
    with jax.named_scope("slots"):
        codes = message.reshape(ROWS, 8, 8, LANES)[:, 0, PIECES - 1, IDX : IDX + 2 * NB].astype(F32)
        slots = (codes[:, NB:] * ROWS + codes[:, :NB]).astype(jnp.int32).reshape(ROWS * NB)
    with jax.named_scope("spread"):
        message, conduct = call(
            spread_body,
            (shape((ROWS, 8, NB * TC), BF16), shape((ROWS, WIDE), F32)),
            [
                pltpu.VMEM((2048, LANES), F32),
                pltpu.VMEM(grid, F32),
                pltpu.VMEM((ROWS + 2, 8, WIDE), F32),
                pltpu.VMEM((BLANK + 1, 8, LANES), F32),
            ],
            1,
        )(slots, message.reshape(2048, LANES))
        message = lax.all_to_all(message, "space", 0, 0, tiled=True)
    with jax.named_scope("observe"):
        message = call(
            observe_body,
            shape((TWP, 8, NB * TC), BF16),
            [pltpu.VMEM((NB, 8, 1536), F32), pltpu.VMEM((NB, 8, 1536), F32)],
        )(message, footprints[0], obs_weight[0])
        message = lax.all_to_all(message, "space", 0, 0, tiled=True)
    with jax.named_scope("collect"):
        message = call(
            collect_body,
            shape((2048, LANES), BF16),
            [
                pltpu.VMEM((2048, LANES), F32),
                pltpu.VMEM(grid, F32),
                pltpu.VMEM((ROWS + 2, 8, WIDE), F32),
                pltpu.VMEM((BLANK + 1, 8, LANES), F32),
            ],
            1,
        )(slots, message, conduct)
        message = lax.all_to_all(message.reshape(256, 8, LANES), both, 0, 0, tiled=True)
    with jax.named_scope("unmix"):
        message = call(
            unmix_body,
            shape((256, WIDE), BF16),
            [pltpu.VMEM((2048, LANES), F32), pltpu.VMEM((256, WIDE), BF16)],
        )(message.reshape(2048, LANES), hi, lo)
        message = lax.all_to_all(message.reshape(8, TWP, WIDE), "tm", 0, 0, tiled=True)
    with jax.named_scope("image"):
        image, sums = call(
            image_body,
            (shape((TW, 8, LON), F32), shape((256, LANES), F32)),
            [pltpu.VMEM((PIECES, 256, LANES), F32)],
        )(message.reshape(256, WIDE), direction, residual)
        sums = lax.all_to_all(sums, both, 0, 0, tiled=True)
    with jax.named_scope("update"):
        outs = call(update_body, tuple(shape((TW, 8, LON), F32) for _ in range(3)))(
            sums, iterate, residual, direction, image
        )
    return tuple(jnp.transpose(value, (1, 0, 2)) for value in outs)


def solution(mesh):
    return jax.shard_map(
        local,
        mesh=mesh,
        in_specs=(
            P(None, "tm", "space"),
            P(None, "tm", "space"),
            P(None, "tm", "space"),
            P("space"),
            P(),
            P("tm", "space"),
            P("tm", "space", None, None),
            P("tm", "space", None),
        ),
        out_specs=(P(None, "tm", "space"), P(None, "tm", "space"), P(None, "tm", "space")),
        check_vma=False,
    )
```

```python
import jax
import jax.numpy as jnp
from jax import lax
from jax.experimental import pallas as pl
from jax.experimental.pallas import tpu as pltpu
from jax.sharding import PartitionSpec as P

LON = 720
TC = 48
NB = 8
DIFF = 2
LANES = 128
WIDE = 768
PIECES = WIDE // LANES
ROWS = 32
TW = 30
TWP = 32
NW = 8
COLS = LON // TC
BLANK = COLS * ROWS
TAIL = LON - (PIECES - 1) * LANES
IDX = 82
F32 = jnp.float32
BF16 = jnp.bfloat16


def call(body, outs, scratch=(), places="", out_places=None):
    space = {"v": pltpu.VMEM, "s": pltpu.SMEM, "h": pltpu.HBM}

    def run(*args):
        kinds = places + "v" * (len(args) - len(places))
        more = {}
        if out_places is not None:
            more["out_specs"] = tuple(pl.BlockSpec(memory_space=space[kind]) for kind in out_places)
        return pl.pallas_call(
            body,
            out_shape=outs,
            in_specs=[pl.BlockSpec(memory_space=space[kind]) for kind in kinds],
            scratch_shapes=list(scratch),
            compiler_params=pltpu.CompilerParams(vmem_limit_bytes=40 * 1024 * 1024),
            **more,
        )(*args)

    return run


def lanes_of(shape):
    return lax.broadcasted_iota(jnp.int32, shape, len(shape) - 1)


def turn(value, shift):
    shift = shift % value.shape[-1]
    return value if shift == 0 else pltpu.roll(value, shift, value.ndim - 1)


def span(start, source, length=TC):
    parts = []
    done = 0
    while done < length:
        a, b = (source + done) // LANES, (start + done) // LANES
        take = min(length - done, (a + 1) * LANES - source - done, (b + 1) * LANES - start - done)
        low = start + done - b * LANES
        parts.append((a, b, low, low + take, (start - source) % LANES))
        done += take
    return parts


def chain(parts, lane, below=None):
    parts = sorted(parts, key=lambda part: part[0])
    result = parts[-1][2]
    for low, high, value in reversed(parts[:-1]):
        result = jnp.where(lane < high, value, result)
    return result


def prepare_body(tile_hbm, d_hbm, out_ref, z_ref, d_ref, tail_ref, tile_ref, sem, tile_sem):
    count = 6
    rows = 240 // count
    copies = [
        pltpu.make_async_copy(d_hbm.at[pl.ds(i * rows, rows)], d_ref.at[pl.ds(i * rows, rows)], sem.at[i])
        for i in range(count)
    ]
    tile_copy = pltpu.make_async_copy(tile_hbm, tile_ref, tile_sem)
    for copy in copies:
        copy.start()
    tile_copy.start()
    lane = lanes_of((rows, LANES))
    for q in range(PIECES - 1):
        z_ref[q, 240:256, :] = jnp.zeros((16, LANES), F32)
    z_ref[PIECES - 1, 248:256, :] = jnp.zeros((8, LANES), F32)
    for i in range(count):
        copies[i].wait()
        at = pl.ds(i * rows, rows)
        tail_ref[at, 0:TAIL] = d_ref[at, (PIECES - 1) * LANES : LON]
        for q in range(PIECES - 1):
            z_ref[q, at, :] = d_ref[at, q * LANES : (q + 1) * LANES]
        tail = tail_ref[at, :]
        first = d_ref[at, 0:LANES]
        z_ref[PIECES - 1, at, :] = jnp.where(
            lane < TAIL,
            tail,
            jnp.where(lane < TAIL + 2, turn(first, TAIL), jnp.where(lane >= LANES - 2, turn(tail, TC), 0.0)),
        )
    tile_copy.wait()
    line = lanes_of((8, LANES))
    codes = jnp.zeros((8, LANES), F32)
    for j in range(NB):
        tile = tile_ref[0, j]
        there = tile >= 0
        safe = jnp.maximum(tile, 0)
        row = (safe * 4370) >> 16
        col = safe - row * COLS
        row = jnp.where(there, row, 0).astype(F32)
        col = jnp.where(there, col, COLS).astype(F32)
        codes = jnp.where(line == IDX + j, row, codes)
        codes = jnp.where(line == IDX + NB + j, col, codes)
    z_ref[PIECES - 1, 240:248, :] = codes
    for q in range(PIECES):
        for k in range(8):
            out_ref[k, :, q * LANES : (q + 1) * LANES] = z_ref.at[q][pl.ds(k, TWP, stride=8), :].astype(BF16)


def factor_body(factor_ref, hi_ref, lo_ref, wide_ref, deep_ref):
    wide_ref[:, LANES:] = jnp.zeros((240, LANES), F32)
    wide_ref[:, 0:240] = factor_ref[...]
    factor = wide_ref[...]
    column = lanes_of((240, 256))
    padded = jnp.zeros((240, 256), F32)
    for w in range(NW):
        here = ((column >> 5) == w) & ((column & 31) < TW)
        padded = jnp.where(here, turn(factor, 2 * w), padded)
    wide_ref[...] = padded
    deep_ref[...] = jnp.zeros((256, 256), F32)
    for w in range(NW):
        deep_ref[TWP * w : TWP * w + TW, :] = wide_ref[TW * w : TW * w + TW, :]
    rows = lax.broadcasted_iota(jnp.int32, (256, 256), 0)
    column = lanes_of((256, 256))
    codes_here = ((column & 31) == TW) & ((rows >> 5) == (column >> 5)) & ((rows & 31) < TW)
    full = jnp.where(codes_here, 1.0, deep_ref[...])
    hi = full.astype(BF16)
    hi_ref[...] = hi
    lo_ref[...] = (full - hi.astype(F32)).astype(BF16)


def mix_body(x_ref, hi_ref, lo_ref, conduct_ref, out_ref, z_ref, k_ref, row_ref):
    x = x_ref[...]
    mixed = jnp.dot(hi_ref[...], x, preferred_element_type=F32) + jnp.dot(
        lo_ref[...], x, preferred_element_type=F32
    )
    for w in range(NW):
        for q in range(PIECES):
            z_ref[pl.ds(w * 8 + q, TWP, stride=64), :] = mixed[TWP * w : TWP * (w + 1), q * LANES : (q + 1) * LANES]
    lane = lanes_of((1, LANES))
    row_ref[...] = jnp.zeros((8, LANES), F32)
    row_ref[0:1, 0:TAIL] = conduct_ref[0:1, (PIECES - 1) * LANES : LON]
    tail = row_ref[0:1, :]
    first = conduct_ref[0:1, 0:LANES]
    last = jnp.where(
        lane < TAIL,
        tail,
        jnp.where(lane < TAIL + 2, turn(first, TAIL), jnp.where(lane >= LANES - 2, turn(tail, TC), 0.0)),
    )
    k_ref[...] = jnp.zeros((16, LANES), F32)
    for q in range(PIECES):
        part = last if q == PIECES - 1 else conduct_ref[0:1, q * LANES : (q + 1) * LANES]
        hi = part.astype(BF16).astype(F32)
        k_ref[q : q + 1, :] = hi
        k_ref[PIECES + q : PIECES + q + 1, :] = part - hi
    m = lax.axis_index("tm")
    for e in range(2):
        part = k_ref[pl.ds(2 * m + e, 1), :]
        z_ref[pl.ds(6 + e, 256, stride=8), :] = jnp.broadcast_to(part, (256, LANES))
    out_ref[...] = z_ref[...].astype(BF16)


def sweep(load, k_ref, store):
    before, here, conduct = None, load(0), k_ref[0:1, :]
    u = here * conduct
    for s in range(ROWS):
        laplace = turn(u, 1) + turn(u, -1) - 4.0 * u
        if before is not None:
            laplace = laplace + before
        if s + 1 < ROWS:
            after, conduct_after = load(s + 1), k_ref[s + 1 : s + 2, :]
            u_after = after * conduct_after
            laplace = laplace + u_after
        store(s, here + conduct * laplace)
        if s + 1 < ROWS:
            before, here, conduct, u = u, after, conduct_after, u_after


def piece(value, q):
    return value[:, q * LANES : (q + 1) * LANES]


def spread_body(slot_ref, x_ref, out_ref, kept_ref, z_ref, w_ref, table_ref):
    lane = lanes_of((8, LANES))
    z_ref[...] = x_ref[...].astype(F32)
    for q in range(PIECES):
        hi, lo = q, PIECES + q
        kept_ref[:, q * LANES : (q + 1) * LANES] = (
            z_ref[pl.ds((hi // 2) * 8 + 6 + hi % 2, ROWS, stride=64), :]
            + z_ref[pl.ds((lo // 2) * 8 + 6 + lo % 2, ROWS, stride=64), :]
        )

    def arrived(s):
        return jnp.concatenate([z_ref[pl.ds(s * 64 + q, 8, stride=8), :] for q in range(PIECES)], axis=1)

    def keep(s, value):
        w_ref[s] = value

    def cut(s, value):
        for c in range(COLS):
            parts = [
                (low, high, turn(piece(value, a), rotation)) for a, _, low, high, rotation in span(0, c * TC)
            ]
            table_ref[c * ROWS + s] = chain(parts, lane)

    sweep(arrived, kept_ref, keep)
    sweep(lambda s: w_ref[s], kept_ref, keep)
    for s in range(ROWS):
        cut(s, w_ref[s])
    table_ref[BLANK] = jnp.zeros((8, LANES), F32)

    ahead = 2
    waiting = {}
    for s in range(ROWS + ahead):
        if s < ROWS:
            waiting[s] = [table_ref[slot_ref[s * NB + j]] for j in range(NB)]
        if s >= ahead:
            tiles = waiting.pop(s - ahead)
            runs = [[], [], []]
            for j in range(NB):
                for _, b, low, high, rotation in span(j * TC, 0):
                    runs[b].append((low, high, turn(tiles[j], rotation)))
            for b in range(3):
                out_ref[s - ahead, :, b * LANES : (b + 1) * LANES] = chain(runs[b], lane).astype(BF16)


def observe_body(x_ref, f_ref, weight_ref, out_ref, x2_ref, g_ref):
    lane = lanes_of((8, LANES))
    runs = {}
    for tau in range(TW):
        value = x_ref[tau].astype(F32)
        for j in range(NB):
            for a, b, low, high, rotation in span(tau * TC, j * TC):
                piece = turn(value[:, a * LANES : (a + 1) * LANES], rotation)
                runs.setdefault((j, b), []).append((low, high, piece))
        for key in [key for key in runs if (key[1] + 1) * LANES <= (tau + 1) * TC or tau == TW - 1]:
            j, b = key
            x2_ref[j, :, b * LANES : (b + 1) * LANES] = chain(runs.pop(key), lane)
    total = jnp.zeros((8, 64), F32)
    for j in range(NB):
        total = total + lax.dot_general(
            x2_ref[j, :, 0 : TW * TC].astype(BF16),
            f_ref[j],
            (((1,), (1,)), ((), ())),
            preferred_element_type=F32,
        )
    weighted = (weight_ref[...] * total).astype(BF16)
    for j in range(NB):
        g_ref[j, :, 0 : TW * TC] = jnp.dot(weighted, f_ref[j], preferred_element_type=F32)
    for tau in range(TW):
        runs = [[], [], []]
        for j in range(NB):
            for a, b, low, high, rotation in span(j * TC, tau * TC):
                runs[b].append((low, high, turn(g_ref[j, :, a * LANES : (a + 1) * LANES], rotation)))
        for b in range(3):
            out_ref[tau, :, b * LANES : (b + 1) * LANES] = chain(runs[b], lane).astype(BF16)
    out_ref[TW:TWP] = jnp.zeros((TWP - TW, 8, NB * TC), BF16)


def collect_body(slot_ref, x_ref, k_ref, out_ref, z_ref, w_ref, table_ref):
    lane = lanes_of((8, LANES))
    table_ref[...] = jnp.zeros(table_ref.shape, F32)

    def reader(s, carry):
        value = x_ref[s].astype(F32)
        tiles = [slot_ref[s * NB + j] for j in range(NB)]
        sums = []
        for j in range(NB):
            parts = [(low, high, turn(piece(value, a), rotation)) for a, _, low, high, rotation in span(0, j * TC)]
            sums.append(table_ref[tiles[j]] + chain(parts, lane))
        for j in range(NB):
            table_ref[tiles[j]] = sums[j]
        return carry

    lax.fori_loop(0, ROWS, reader, 0, unroll=True)

    def joined(s):
        runs = [[] for _ in range(PIECES)]
        for c in range(COLS):
            tile = table_ref[c * ROWS + s]
            for _, b, low, high, rotation in span(c * TC, 0):
                runs[b].append((low, high, turn(tile, rotation)))
        runs[-1].append((TAIL, TAIL + 2, turn(table_ref[s], TAIL)))
        runs[-1].append((TAIL + 2, LANES - 2, jnp.zeros((8, LANES), F32)))
        runs[-1].append((LANES - 2, LANES, turn(table_ref[(COLS - 1) * ROWS + s], TAIL)))
        return jnp.concatenate([chain(run, lane) for run in runs], axis=1)

    def keep(s, value):
        w_ref[s] = value

    def leave(s, value):
        for q in range(PIECES):
            z_ref[pl.ds(s * 8 * PIECES + q, 8, stride=PIECES), :] = piece(value, q)

    for s in range(ROWS):
        keep(s, joined(s))
    for _ in range(DIFF):
        sweep(lambda s: w_ref[s], k_ref, keep)
    for s in range(ROWS):
        leave(s, w_ref[s])
    out_ref[...] = z_ref[...].astype(BF16)


def unmix_body(x_ref, hi_ref, lo_ref, out_ref, z_ref, w_ref):
    z_ref[...] = x_ref[...].astype(F32)
    for w in range(NW):
        for q in range(PIECES):
            w_ref[TWP * w : TWP * (w + 1), q * LANES : (q + 1) * LANES] = z_ref[
                pl.ds(w * PIECES + q, TWP, stride=NW * PIECES), :
            ].astype(BF16)
    x = w_ref[...]
    down = (((0,), (0,)), ((), ()))
    mixed = lax.dot_general(hi_ref[...], x, down, preferred_element_type=F32) + lax.dot_general(
        lo_ref[...], x, down, preferred_element_type=F32
    )
    out_ref[...] = mixed.astype(BF16)


def image_body(x_ref, d_ref, r_ref, image_ref, sums_ref, z_ref):
    for q in range(PIECES):
        z_ref[q] = x_ref[:, q * LANES : (q + 1) * LANES].astype(F32)
    totals = [jnp.zeros((8, 1), F32) for _ in range(4)]
    for q in range(PIECES):
        width = TAIL if q == PIECES - 1 else LANES
        at = pl.ds(q * LANES, width)
        sums = [jnp.zeros((8, width), F32) for _ in range(4)]
        for t in range(TW):
            d = d_ref[t, :, at]
            r = r_ref[t, :, at]
            image = d + z_ref.at[q][pl.ds(t, 8, stride=TWP), :][:, 0:width]
            image_ref[t, :, at] = image
            for i, (left, right) in enumerate(((r, r), (d, image), (r, image), (image, image))):
                sums[i] = sums[i] + left * right
        for i in range(4):
            totals[i] = totals[i] + jnp.sum(sums[i], axis=1, keepdims=True)
    lane = lanes_of((8, LANES))
    k = lax.broadcasted_iota(jnp.int32, (8, LANES), 0)
    spread = jnp.zeros((8, LANES), F32)
    for i in range(4):
        spread = jnp.where(lane == k * 4 + i, totals[i], spread)
    line = jnp.sum(spread, axis=0, keepdims=True)
    sums_ref[...] = jnp.broadcast_to(line, sums_ref.shape)


def update_body(sums_ref, it_ref, r_ref, d_ref, image_ref, it_out, r_out, d_out, it_new, r_new, d_new, sem):
    line = jnp.sum(sums_ref[...], axis=0, keepdims=True)
    lane = lanes_of((8, LANES))
    k = lax.broadcasted_iota(jnp.int32, (8, LANES), 0)
    rr, dq, rq, qq = [
        jnp.sum(jnp.where(lane == k * 4 + i, line, 0.0), axis=1, keepdims=True) for i in range(4)
    ]
    step = rr / dq
    norm = jnp.maximum(rr + step * (step * qq - 2.0 * rq), 0.0)
    ratio = norm / rr
    count = 5
    rows = TW // count
    copies = []
    for i in range(count):
        for t in range(i * rows, (i + 1) * rows):
            d = d_ref[t]
            after = r_ref[t] - step * image_ref[t]
            it_new[t] = it_ref[t] + step * d
            r_new[t] = after
            d_new[t] = after + ratio * d
        at = pl.ds(i * rows, rows)
        for n, (new, out) in enumerate(((it_new, it_out), (r_new, r_out), (d_new, d_out))):
            copies.append(pltpu.make_async_copy(new.at[at], out.at[at], sem.at[n, i]))
            copies[-1].start()
    for copy in copies:
        copy.wait()


def shape(dims, dtype):
    return jax.ShapeDtypeStruct(dims, dtype)


def local(
    iterate, residual, direction, diffusivity, temporal_factor, block_tile, footprints, obs_weight
):
    both = ("space", "tm")
    iterate, residual, direction = [
        jnp.transpose(value, (1, 0, 2)) for value in (iterate, residual, direction)
    ]
    grid = (ROWS, 8, WIDE)
    with jax.named_scope("prepare"):
        message = call(
            prepare_body,
            shape((8, TWP, WIDE), BF16),
            [
                pltpu.VMEM((PIECES, 256, LANES), F32),
                pltpu.VMEM((240, LON), F32),
                pltpu.VMEM((240, LANES), F32),
                pltpu.SMEM((1, NB), jnp.int32),
                pltpu.SemaphoreType.DMA((6,)),
                pltpu.SemaphoreType.DMA,
            ],
            "hh",
        )(
            pltpu.with_memory_space_constraint(block_tile, pltpu.HBM),
            pltpu.with_memory_space_constraint(direction.reshape(240, LON), pltpu.HBM),
        )
        message = lax.all_to_all(message, "tm", 0, 0, tiled=True)
    with jax.named_scope("factor"):
        hi, lo = call(
            factor_body,
            (shape((256, 256), BF16), shape((256, 256), BF16)),
            [pltpu.VMEM((240, 256), F32), pltpu.VMEM((256, 256), F32)],
        )(temporal_factor)
    with jax.named_scope("mix"):
        message = call(
            mix_body,
            shape((2048, LANES), BF16),
            [pltpu.VMEM((2048, LANES), F32), pltpu.VMEM((16, LANES), F32), pltpu.VMEM((8, LANES), F32)],
        )(message.reshape(256, WIDE), hi, lo, diffusivity.reshape(1, LON))
        message = lax.all_to_all(message.reshape(256, 8, LANES), both, 0, 0, tiled=True)
    with jax.named_scope("slots"):
        codes = message.reshape(ROWS, 8, 8, LANES)[:, 0, PIECES - 1, IDX : IDX + 2 * NB].astype(F32)
        slots = (codes[:, NB:] * ROWS + codes[:, :NB]).astype(jnp.int32).reshape(ROWS * NB)
    with jax.named_scope("spread"):
        message, conduct = call(
            spread_body,
            (shape((ROWS, 8, NB * TC), BF16), shape((ROWS, WIDE), F32)),
            [
                pltpu.VMEM((2048, LANES), F32),
                pltpu.VMEM(grid, F32),
                pltpu.VMEM((BLANK + 1, 8, LANES), F32),
            ],
            "s",
        )(slots, message.reshape(2048, LANES))
        message = lax.all_to_all(message, "space", 0, 0, tiled=True)
    with jax.named_scope("observe"):
        message = call(
            observe_body,
            shape((TWP, 8, NB * TC), BF16),
            [pltpu.VMEM((NB, 8, 1536), F32), pltpu.VMEM((NB, 8, 1536), F32)],
        )(message, footprints[0], obs_weight[0])
        message = lax.all_to_all(message, "space", 0, 0, tiled=True)
    with jax.named_scope("collect"):
        message = call(
            collect_body,
            shape((1536, LANES), BF16),
            [
                pltpu.VMEM((1536, LANES), F32),
                pltpu.VMEM(grid, F32),
                pltpu.VMEM((BLANK + 1, 8, LANES), F32),
            ],
            "s",
        )(slots, message, conduct)
        message = lax.all_to_all(message.reshape(768, 2, LANES), both, 0, 0, tiled=True)
    with jax.named_scope("unmix"):
        message = call(
            unmix_body,
            shape((256, WIDE), BF16),
            [pltpu.VMEM((1536, LANES), F32), pltpu.VMEM((256, WIDE), BF16)],
        )(message.reshape(1536, LANES), hi, lo)
        message = lax.all_to_all(message.reshape(8, TWP, WIDE), "tm", 0, 0, tiled=True)
    with jax.named_scope("image"):
        image, sums = call(
            image_body,
            (shape((TW, 8, LON), F32), shape((256, LANES), F32)),
            [pltpu.VMEM((PIECES, 256, LANES), F32)],
        )(message.reshape(256, WIDE), direction, residual)
        sums = lax.all_to_all(sums, both, 0, 0, tiled=True)
    with jax.named_scope("update"):
        whole = (TW, 8, LON)
        outs = call(
            update_body,
            tuple(shape(whole, F32) for _ in range(3)),
            [pltpu.VMEM(whole, F32) for _ in range(3)] + [pltpu.SemaphoreType.DMA((3, 5))],
            out_places="hhh",
        )(sums, iterate, residual, direction, image)
    return tuple(jnp.transpose(value, (1, 0, 2)) for value in outs)


def solution(mesh):
    return jax.shard_map(
        local,
        mesh=mesh,
        in_specs=(
            P(None, "tm", "space"),
            P(None, "tm", "space"),
            P(None, "tm", "space"),
            P("space"),
            P(),
            P("tm", "space"),
            P("tm", "space", None, None),
            P("tm", "space", None),
        ),
        out_specs=(P(None, "tm", "space"), P(None, "tm", "space"), P(None, "tm", "space")),
        check_vma=False,
    )
```

```python
import jax
import jax.numpy as jnp
from jax import lax
from jax.experimental import pallas as pl
from jax.experimental.pallas import tpu as pltpu
from jax.sharding import PartitionSpec as P

LON = 720
TC = 48
NB = 8
DIFF = 2
LANES = 128
WIDE = 768
PIECES = WIDE // LANES
ROWS = 32
TW = 30
TWP = 32
NW = 8
COLS = LON // TC
BLANK = COLS * ROWS
TAIL = LON - (PIECES - 1) * LANES
IDX = 82
F32 = jnp.float32
BF16 = jnp.bfloat16


def call(body, outs, scratch=(), places="", out_places=None):
    space = {"v": pltpu.VMEM, "s": pltpu.SMEM, "h": pltpu.HBM}

    def run(*args):
        kinds = places + "v" * (len(args) - len(places))
        more = {}
        if out_places is not None:
            more["out_specs"] = tuple(pl.BlockSpec(memory_space=space[kind]) for kind in out_places)
        return pl.pallas_call(
            body,
            out_shape=outs,
            in_specs=[pl.BlockSpec(memory_space=space[kind]) for kind in kinds],
            scratch_shapes=list(scratch),
            compiler_params=pltpu.CompilerParams(vmem_limit_bytes=40 * 1024 * 1024),
            **more,
        )(*args)

    return run


def lanes_of(shape):
    return lax.broadcasted_iota(jnp.int32, shape, len(shape) - 1)


def turn(value, shift):
    shift = shift % value.shape[-1]
    return value if shift == 0 else pltpu.roll(value, shift, value.ndim - 1)


def span(start, source, length=TC):
    parts = []
    done = 0
    while done < length:
        a, b = (source + done) // LANES, (start + done) // LANES
        take = min(length - done, (a + 1) * LANES - source - done, (b + 1) * LANES - start - done)
        low = start + done - b * LANES
        parts.append((a, b, low, low + take, (start - source) % LANES))
        done += take
    return parts


def chain(parts, lane, below=None):
    parts = sorted(parts, key=lambda part: part[0])
    result = parts[-1][2]
    for low, high, value in reversed(parts[:-1]):
        result = jnp.where(lane < high, value, result)
    return result


def wrapped(first, tail, lane):
    return jnp.where(
        lane < TAIL,
        tail,
        jnp.where(lane < TAIL + 2, turn(first, TAIL), jnp.where(lane >= LANES - 2, turn(tail, TC), 0.0)),
    )


def prepare_body(
    tile_hbm, d_hbm, factor_hbm, conduct_hbm, out_ref, hi_ref, lo_ref, cut_ref,
    z_ref, tail_ref, wide_tail_ref, tile_ref, factor_ref, wide_ref, deep_ref, conduct_ref, row_ref, sem, more_sem,
):
    factor_copy = pltpu.make_async_copy(factor_hbm, factor_ref, more_sem.at[0])
    tile_copy = pltpu.make_async_copy(tile_hbm, tile_ref, more_sem.at[1])
    conduct_copy = pltpu.make_async_copy(conduct_hbm, conduct_ref, more_sem.at[2])
    last = PIECES - 1
    copies = [
        pltpu.make_async_copy(
            d_hbm.at[:, pl.ds(q * LANES, LANES)], z_ref.at[q, pl.ds(0, 240), :], sem.at[q]
        )
        for q in range(last)
    ] + [pltpu.make_async_copy(d_hbm.at[:, pl.ds(last * LANES, TAIL)], tail_ref, sem.at[last])]
    factor_copy.start()
    for copy in copies:
        copy.start()
    tile_copy.start()
    conduct_copy.start()
    for q in range(PIECES - 1):
        z_ref[q, 240:256, :] = jnp.zeros((16, LANES), F32)
    z_ref[PIECES - 1, 248:256, :] = jnp.zeros((8, LANES), F32)
    deep_ref[...] = jnp.zeros((256, 256), F32)
    wide_ref[:, LANES:] = jnp.zeros((240, LANES), F32)
    factor_copy.wait()
    wide_ref[:, 0:240] = factor_ref[...]
    factor = wide_ref[...]
    line = lanes_of((240, LANES))
    runs = [[], []]
    for w in range(NW):
        for a, b, low, high, rotation in span(TWP * w, TW * w, TW):
            runs[b].append((low, high, turn(piece(factor, a), rotation)))
        low = TWP * w % LANES + TW
        runs[TWP * w // LANES].append((low, low + TWP - TW, jnp.zeros((240, LANES), F32)))
    for b in range(2):
        wide_ref[:, b * LANES : (b + 1) * LANES] = chain(runs[b], line)
    for w in range(NW):
        deep_ref[TWP * w : TWP * w + TW, :] = wide_ref[TW * w : TW * w + TW, :]
    row = lax.broadcasted_iota(jnp.int32, (256, 256), 0)
    column = lanes_of((256, 256))
    codes_here = ((column & 31) == TW) & ((row >> 5) == (column >> 5)) & ((row & 31) < TW)
    full = jnp.where(codes_here, 1.0, deep_ref[...])
    hi = full.astype(BF16)
    hi_ref[...] = hi
    lo_ref[...] = (full - hi.astype(F32)).astype(BF16)
    copies[last].wait()
    copies[0].wait()
    wide_tail_ref[:, 0:TAIL] = tail_ref[...]
    z_ref[last, 0:240, :] = wrapped(z_ref[0, 0:240, :], wide_tail_ref[...], lanes_of((240, LANES)))
    tile_copy.wait()
    line = lanes_of((8, LANES))
    codes = jnp.zeros((8, LANES), F32)
    for j in range(NB):
        tile = tile_ref[0, j]
        there = tile >= 0
        safe = jnp.maximum(tile, 0)
        row = (safe * 4370) >> 16
        col = safe - row * COLS
        row = jnp.where(there, row, 0).astype(F32)
        col = jnp.where(there, col, COLS).astype(F32)
        codes = jnp.where(line == IDX + j, row, codes)
        codes = jnp.where(line == IDX + NB + j, col, codes)
    z_ref[PIECES - 1, 240:248, :] = codes
    conduct_copy.wait()
    lane = lanes_of((1, LANES))
    row_ref[...] = jnp.zeros((8, LANES), F32)
    row_ref[0:1, 0:TAIL] = conduct_ref[pl.ds((PIECES - 1) * LANES, TAIL)].reshape(1, TAIL)
    cut_ref[...] = jnp.zeros((16, LANES), F32)
    for q in range(PIECES):
        if q < PIECES - 1:
            part = conduct_ref[pl.ds(q * LANES, LANES)].reshape(1, LANES)
        else:
            part = wrapped(conduct_ref[pl.ds(0, LANES)].reshape(1, LANES), row_ref[0:1, :], lane)
        hi = part.astype(BF16).astype(F32)
        cut_ref[q : q + 1, :] = hi
        cut_ref[PIECES + q : PIECES + q + 1, :] = part - hi
    for q in range(PIECES):
        if 0 < q < last:
            copies[q].wait()
        for k in range(8):
            out_ref[k, :, q * LANES : (q + 1) * LANES] = z_ref.at[q][pl.ds(k, TWP, stride=8), :].astype(BF16)


def mix_body(x_ref, hi_ref, lo_ref, cut_ref, out_ref, z_ref):
    x = x_ref[...]
    mixed = jnp.dot(hi_ref[...], x, preferred_element_type=F32) + jnp.dot(
        lo_ref[...], x, preferred_element_type=F32
    )
    m = lax.axis_index("tm")
    for e in range(2):
        part = cut_ref[pl.ds(2 * m + e, 1), :]
        z_ref[pl.ds(PIECES + e, 256, stride=8), :] = jnp.broadcast_to(part, (256, LANES))
    for w in range(NW):
        for q in range(PIECES):
            z_ref[pl.ds(w * 8 + q, TWP, stride=64), :] = mixed[TWP * w : TWP * (w + 1), q * LANES : (q + 1) * LANES]
    out_ref[...] = z_ref[0:2048, :].astype(BF16)


def sweep(load, k_ref, store):
    before, here, conduct = None, load(0), k_ref[0:1, :]
    u = here * conduct
    for s in range(ROWS):
        laplace = turn(u, 1) + turn(u, -1) - 4.0 * u
        if before is not None:
            laplace = laplace + before
        if s + 1 < ROWS:
            after, conduct_after = load(s + 1), k_ref[s + 1 : s + 2, :]
            u_after = after * conduct_after
            laplace = laplace + u_after
        store(s, here + conduct * laplace)
        if s + 1 < ROWS:
            before, here, conduct, u = u, after, conduct_after, u_after


def piece(value, q):
    return value[:, q * LANES : (q + 1) * LANES]


def spread_body(x_ref, out_ref, kept_ref, code_ref, z_ref, w_ref, table_ref, slot_ref, sem):
    lane = lanes_of((8, LANES))
    z_ref[0:2048, :] = x_ref[...].astype(F32)
    codes = z_ref[pl.ds(PIECES - 1, ROWS, stride=64), :]
    line = lanes_of((ROWS, LANES))
    codes = jnp.where((line >= IDX) & (line < IDX + NB), turn(codes, -NB) * ROWS + codes, 0.0)
    code_ref[...] = codes.astype(jnp.int32)
    slot_copy = pltpu.make_async_copy(code_ref, slot_ref, sem)
    slot_copy.start()
    for q in range(PIECES):
        hi, lo = q, PIECES + q
        kept_ref[:, q * LANES : (q + 1) * LANES] = (
            z_ref[pl.ds((hi // 2) * 8 + 6 + hi % 2, ROWS, stride=64), :]
            + z_ref[pl.ds((lo // 2) * 8 + 6 + lo % 2, ROWS, stride=64), :]
        )

    def arrived(s):
        return jnp.concatenate([z_ref[pl.ds(s * 64 + q, 8, stride=8), :] for q in range(PIECES)], axis=1)

    def keep(s, value):
        w_ref[s] = value

    def cut(s, value):
        for c in range(COLS):
            parts = [
                (low, high, turn(piece(value, a), rotation)) for a, _, low, high, rotation in span(0, c * TC)
            ]
            table_ref[c * ROWS + s] = chain(parts, lane)

    sweep(arrived, kept_ref, keep)
    sweep(lambda s: w_ref[s], kept_ref, keep)
    for s in range(ROWS):
        cut(s, w_ref[s])
    table_ref[BLANK] = jnp.zeros((8, LANES), F32)

    slot_copy.wait()
    ahead = 2
    waiting = {}
    for s in range(ROWS + ahead):
        if s < ROWS:
            waiting[s] = [table_ref[slot_ref[s, IDX + j]] for j in range(NB)]
        if s >= ahead:
            tiles = waiting.pop(s - ahead)
            runs = [[], [], []]
            for j in range(NB):
                for _, b, low, high, rotation in span(j * TC, 0):
                    runs[b].append((low, high, turn(tiles[j], rotation)))
            for b in range(3):
                out_ref[s - ahead, :, b * LANES : (b + 1) * LANES] = chain(runs[b], lane).astype(BF16)


def observe_body(x_ref, f_ref, weight_ref, out_ref, x2_ref, g_ref):
    lane = lanes_of((8, LANES))
    runs = {}
    for tau in range(TW):
        value = x_ref[tau].astype(F32)
        for j in range(NB):
            for a, b, low, high, rotation in span(tau * TC, j * TC):
                piece = turn(value[:, a * LANES : (a + 1) * LANES], rotation)
                runs.setdefault((j, b), []).append((low, high, piece))
        for key in [key for key in runs if (key[1] + 1) * LANES <= (tau + 1) * TC or tau == TW - 1]:
            j, b = key
            x2_ref[j, :, b * LANES : (b + 1) * LANES] = chain(runs.pop(key), lane)
    total = jnp.zeros((8, 64), F32)
    for j in range(NB):
        total = total + lax.dot_general(
            x2_ref[j, :, 0 : TW * TC].astype(BF16),
            f_ref[j],
            (((1,), (1,)), ((), ())),
            preferred_element_type=F32,
        )
    weighted = (weight_ref[...] * total).astype(BF16)
    for j in range(NB):
        g_ref[j, :, 0 : TW * TC] = jnp.dot(weighted, f_ref[j], preferred_element_type=F32)
    for tau in range(TW):
        runs = [[], [], []]
        for j in range(NB):
            for a, b, low, high, rotation in span(j * TC, tau * TC):
                runs[b].append((low, high, turn(g_ref[j, :, a * LANES : (a + 1) * LANES], rotation)))
        for b in range(3):
            out_ref[tau, :, b * LANES : (b + 1) * LANES] = chain(runs[b], lane).astype(BF16)
    out_ref[TW:TWP] = jnp.zeros((TWP - TW, 8, NB * TC), BF16)


def collect_body(slot_any, x_ref, k_ref, out_ref, z_ref, w_ref, table_ref, slot_ref, sem):
    slot_copy = pltpu.make_async_copy(slot_any, slot_ref, sem)
    slot_copy.start()
    lane = lanes_of((8, LANES))
    table_ref[...] = jnp.zeros(table_ref.shape, F32)
    slot_copy.wait()

    def reader(s, carry):
        value = x_ref[s].astype(F32)
        tiles = [slot_ref[s, IDX + j] for j in range(NB)]
        sums = []
        for j in range(NB):
            parts = [(low, high, turn(piece(value, a), rotation)) for a, _, low, high, rotation in span(0, j * TC)]
            sums.append(table_ref[tiles[j]] + chain(parts, lane))
        for j in range(NB):
            table_ref[tiles[j]] = sums[j]
        return carry

    lax.fori_loop(0, ROWS, reader, 0, unroll=True)

    def joined(s):
        runs = [[] for _ in range(PIECES)]
        for c in range(COLS):
            tile = table_ref[c * ROWS + s]
            for _, b, low, high, rotation in span(c * TC, 0):
                runs[b].append((low, high, turn(tile, rotation)))
        runs[-1].append((TAIL, TAIL + 2, turn(table_ref[s], TAIL)))
        runs[-1].append((TAIL + 2, LANES - 2, jnp.zeros((8, LANES), F32)))
        runs[-1].append((LANES - 2, LANES, turn(table_ref[(COLS - 1) * ROWS + s], TAIL)))
        return jnp.concatenate([chain(run, lane) for run in runs], axis=1)

    def keep(s, value):
        w_ref[s] = value

    def leave(s, value):
        for q in range(PIECES):
            z_ref[pl.ds(s * 8 * PIECES + q, 8, stride=PIECES), :] = piece(value, q)

    for s in range(ROWS):
        keep(s, joined(s))
    for _ in range(DIFF):
        sweep(lambda s: w_ref[s], k_ref, keep)
    for s in range(ROWS):
        leave(s, w_ref[s])
    out_ref[...] = z_ref[0:1536, :].astype(BF16)


def unmix_body(x_ref, hi_ref, lo_ref, out_ref, z_ref, w_ref):
    z_ref[0:1536, :] = x_ref[...].astype(F32)
    for w in range(NW):
        for q in range(PIECES):
            w_ref[TWP * w : TWP * (w + 1), q * LANES : (q + 1) * LANES] = z_ref[
                pl.ds(w * PIECES + q, TWP, stride=NW * PIECES), :
            ].astype(BF16)
    x = w_ref[...]
    down = (((0,), (0,)), ((), ()))
    mixed = lax.dot_general(hi_ref[...], x, down, preferred_element_type=F32) + lax.dot_general(
        lo_ref[...], x, down, preferred_element_type=F32
    )
    out_ref[...] = mixed.astype(BF16)


def image_body(x_ref, d_ref, r_ref, image_ref, sums_ref, z_ref):
    for q in range(PIECES):
        z_ref[q, 0:256, :] = x_ref[:, q * LANES : (q + 1) * LANES].astype(F32)
    totals = [jnp.zeros((8, 1), F32) for _ in range(4)]
    for q in range(PIECES):
        width = TAIL if q == PIECES - 1 else LANES
        at = pl.ds(q * LANES, width)
        sums = [jnp.zeros((8, width), F32) for _ in range(4)]
        for t in range(TW):
            d = d_ref[t, :, at]
            r = r_ref[t, :, at]
            image = d + z_ref.at[q][pl.ds(t, 8, stride=TWP), :][:, 0:width]
            image_ref[t, :, at] = image
            for i, (left, right) in enumerate(((r, r), (d, image), (r, image), (image, image))):
                sums[i] = sums[i] + left * right
        for i in range(4):
            totals[i] = totals[i] + jnp.sum(sums[i], axis=1, keepdims=True)
    lane = lanes_of((8, LANES))
    k = lax.broadcasted_iota(jnp.int32, (8, LANES), 0)
    spread = jnp.zeros((8, LANES), F32)
    for i in range(4):
        spread = jnp.where(lane == k * 4 + i, totals[i], spread)
    line = jnp.sum(spread, axis=0, keepdims=True)
    sums_ref[...] = jnp.broadcast_to(line, sums_ref.shape)


def update_body(sums_ref, it_ref, r_ref, d_ref, image_ref, it_out, r_out, d_out, it_new, r_new, d_new, sem):
    line = jnp.sum(sums_ref[...], axis=0, keepdims=True)
    lane = lanes_of((8, LANES))
    k = lax.broadcasted_iota(jnp.int32, (8, LANES), 0)
    rr, dq, rq, qq = [
        jnp.sum(jnp.where(lane == k * 4 + i, line, 0.0), axis=1, keepdims=True) for i in range(4)
    ]
    step = rr / dq
    norm = jnp.maximum(rr + step * (step * qq - 2.0 * rq), 0.0)
    ratio = norm / rr
    count = 3
    rows = TW // count
    copies = []
    for i in range(count):
        for t in range(i * rows, (i + 1) * rows):
            d = d_ref[t]
            after = r_ref[t] - step * image_ref[t]
            it_new[t] = it_ref[t] + step * d
            r_new[t] = after
            d_new[t] = after + ratio * d
        at = pl.ds(i * rows, rows)
        for n, (new, out) in enumerate(((it_new, it_out), (r_new, r_out), (d_new, d_out))):
            copies.append(pltpu.make_async_copy(new.at[at], out.at[at], sem.at[n, i]))
            copies[-1].start()
    for copy in copies:
        copy.wait()


def shape(dims, dtype):
    return jax.ShapeDtypeStruct(dims, dtype)


def local(
    iterate, residual, direction, diffusivity, temporal_factor, block_tile, footprints, obs_weight
):
    both = ("space", "tm")
    iterate, residual, direction = [
        jnp.transpose(value, (1, 0, 2)) for value in (iterate, residual, direction)
    ]
    grid = (ROWS, 8, WIDE)
    with jax.named_scope("prepare"):
        message, hi, lo, cut = call(
            prepare_body,
            (
                shape((8, TWP, WIDE), BF16),
                shape((256, 256), BF16),
                shape((256, 256), BF16),
                shape((16, LANES), F32),
            ),
            [
                pltpu.VMEM((PIECES, 264, LANES), F32),
                pltpu.VMEM((240, TAIL), F32),
                pltpu.VMEM((240, LANES), F32),
                pltpu.SMEM((1, NB), jnp.int32),
                pltpu.VMEM((240, 240), F32),
                pltpu.VMEM((240, 256), F32),
                pltpu.VMEM((256, 256), F32),
                pltpu.VMEM((LON,), F32),
                pltpu.VMEM((8, LANES), F32),
                pltpu.SemaphoreType.DMA((6,)),
                pltpu.SemaphoreType.DMA((3,)),
            ],
            "hhhh",
        )(
            *[
                pltpu.with_memory_space_constraint(value, pltpu.HBM)
                for value in (block_tile, direction.reshape(240, LON), temporal_factor, diffusivity)
            ]
        )
        message = lax.all_to_all(message, "tm", 0, 0, tiled=True)
    with jax.named_scope("mix"):
        message = call(mix_body, shape((2048, LANES), BF16), [pltpu.VMEM((2112, LANES), F32)])(
            message.reshape(256, WIDE), hi, lo, cut
        )
        message = lax.all_to_all(message.reshape(256, 8, LANES), both, 0, 0, tiled=True)
    with jax.named_scope("spread"):
        message, conduct, slots = call(
            spread_body,
            (shape((ROWS, 8, NB * TC), BF16), shape((ROWS, WIDE), F32), shape((ROWS, LANES), jnp.int32)),
            [
                pltpu.VMEM((2112, LANES), F32),
                pltpu.VMEM(grid, F32),
                pltpu.VMEM((BLANK + 1, 8, LANES), F32),
                pltpu.SMEM((ROWS, LANES), jnp.int32),
                pltpu.SemaphoreType.DMA,
            ],
        )(message.reshape(2048, LANES))
        message = lax.all_to_all(message, "space", 0, 0, tiled=True)
    with jax.named_scope("observe"):
        message = call(
            observe_body,
            shape((TWP, 8, NB * TC), BF16),
            [pltpu.VMEM((NB, 8, 1536), F32), pltpu.VMEM((NB, 8, 1536), F32)],
        )(message, footprints[0], obs_weight[0])
        message = lax.all_to_all(message, "space", 0, 0, tiled=True)
    with jax.named_scope("collect"):
        message = call(
            collect_body,
            shape((1536, LANES), BF16),
            [
                pltpu.VMEM((1584, LANES), F32),
                pltpu.VMEM(grid, F32),
                pltpu.VMEM((BLANK + 1, 8, LANES), F32),
                pltpu.SMEM((ROWS, LANES), jnp.int32),
                pltpu.SemaphoreType.DMA,
            ],
            "h",
        )(slots, message, conduct)
        message = lax.all_to_all(message.reshape(768, 2, LANES), both, 0, 0, tiled=True)
    with jax.named_scope("unmix"):
        message = call(
            unmix_body,
            shape((256, WIDE), BF16),
            [pltpu.VMEM((1584, LANES), F32), pltpu.VMEM((256, WIDE), BF16)],
        )(message.reshape(1536, LANES), hi, lo)
        message = lax.all_to_all(message.reshape(8, TWP, WIDE), "tm", 0, 0, tiled=True)
    with jax.named_scope("image"):
        image, sums = call(
            image_body,
            (shape((TW, 8, LON), F32), shape((256, LANES), F32)),
            [pltpu.VMEM((PIECES, 288, LANES), F32)],
        )(message.reshape(256, WIDE), direction, residual)
        sums = lax.all_to_all(sums, both, 0, 0, tiled=True)
    with jax.named_scope("update"):
        whole = (TW, 8, LON)
        outs = call(
            update_body,
            tuple(shape(whole, F32) for _ in range(3)),
            [pltpu.VMEM(whole, F32) for _ in range(3)] + [pltpu.SemaphoreType.DMA((3, 3))],
            out_places="hhh",
        )(sums, iterate, residual, direction, image)
    return tuple(jnp.transpose(value, (1, 0, 2)) for value in outs)


def solution(mesh):
    return jax.shard_map(
        local,
        mesh=mesh,
        in_specs=(
            P(None, "tm", "space"),
            P(None, "tm", "space"),
            P(None, "tm", "space"),
            P("space"),
            P(),
            P("tm", "space"),
            P("tm", "space", None, None),
            P("tm", "space", None),
        ),
        out_specs=(P(None, "tm", "space"), P(None, "tm", "space"), P(None, "tm", "space")),
        check_vma=False,
    )
```

```python
import jax
import jax.numpy as jnp
from jax import lax
from jax.experimental import pallas as pl
from jax.experimental.pallas import tpu as pltpu
from jax.sharding import PartitionSpec as P

LON = 720
TC = 48
NB = 8
DIFF = 2
LANES = 128
WIDE = 768
PIECES = WIDE // LANES
ROWS = 32
TW = 30
TWP = 32
NW = 8
COLS = LON // TC
BLANK = COLS * ROWS
TAIL = LON - (PIECES - 1) * LANES
IDX = 82
F32 = jnp.float32
BF16 = jnp.bfloat16


def call(body, outs, scratch=(), places="", out_places=None):
    space = {"v": pltpu.VMEM, "s": pltpu.SMEM, "h": pltpu.HBM}

    def run(*args):
        kinds = places + "v" * (len(args) - len(places))
        more = {}
        if out_places is not None:
            more["out_specs"] = tuple(pl.BlockSpec(memory_space=space[kind]) for kind in out_places)
        return pl.pallas_call(
            body,
            out_shape=outs,
            in_specs=[pl.BlockSpec(memory_space=space[kind]) for kind in kinds],
            scratch_shapes=list(scratch),
            compiler_params=pltpu.CompilerParams(vmem_limit_bytes=40 * 1024 * 1024),
            **more,
        )(*args)

    return run


def lanes_of(shape):
    return lax.broadcasted_iota(jnp.int32, shape, len(shape) - 1)


def turn(value, shift):
    shift = shift % value.shape[-1]
    return value if shift == 0 else pltpu.roll(value, shift, value.ndim - 1)


def span(start, source, length=TC):
    parts = []
    done = 0
    while done < length:
        a, b = (source + done) // LANES, (start + done) // LANES
        take = min(length - done, (a + 1) * LANES - source - done, (b + 1) * LANES - start - done)
        low = start + done - b * LANES
        parts.append((a, b, low, low + take, (start - source) % LANES))
        done += take
    return parts


def chain(parts, lane, below=None):
    parts = sorted(parts, key=lambda part: part[0])
    result = parts[-1][2]
    for low, high, value in reversed(parts[:-1]):
        result = jnp.where(lane < high, value, result)
    return result


def wrapped(first, tail, lane):
    return jnp.where(
        lane < TAIL,
        tail,
        jnp.where(lane < TAIL + 2, turn(first, TAIL), jnp.where(lane >= LANES - 2, turn(tail, TC), 0.0)),
    )


def prepare_body(
    tile_hbm, d_hbm, factor_hbm, conduct_hbm, out_ref, hi_ref, lo_ref, cut_ref,
    z_ref, tail_ref, wide_tail_ref, tile_ref, factor_ref, wide_ref, deep_ref, conduct_ref, row_ref, sem, more_sem,
):
    factor_copy = pltpu.make_async_copy(factor_hbm, factor_ref, more_sem.at[0])
    tile_copy = pltpu.make_async_copy(tile_hbm, tile_ref, more_sem.at[1])
    conduct_copy = pltpu.make_async_copy(conduct_hbm, conduct_ref, more_sem.at[2])
    last = PIECES - 1
    copies = [
        pltpu.make_async_copy(
            d_hbm.at[:, pl.ds(q * LANES, LANES)], z_ref.at[q, pl.ds(0, 240), :], sem.at[q]
        )
        for q in range(last)
    ] + [pltpu.make_async_copy(d_hbm.at[:, pl.ds(last * LANES, TAIL)], tail_ref, sem.at[last])]
    factor_copy.start()
    for copy in copies:
        copy.start()
    tile_copy.start()
    conduct_copy.start()
    for q in range(PIECES - 1):
        z_ref[q, 240:256, :] = jnp.zeros((16, LANES), F32)
    z_ref[PIECES - 1, 248:256, :] = jnp.zeros((8, LANES), F32)
    deep_ref[...] = jnp.zeros((256, 256), F32)
    wide_ref[:, LANES:] = jnp.zeros((240, LANES), F32)
    factor_copy.wait()
    wide_ref[:, 0:240] = factor_ref[...]
    factor = wide_ref[...]
    line = lanes_of((240, LANES))
    runs = [[], []]
    for w in range(NW):
        for a, b, low, high, rotation in span(TWP * w, TW * w, TW):
            runs[b].append((low, high, turn(piece(factor, a), rotation)))
        low = TWP * w % LANES + TW
        runs[TWP * w // LANES].append((low, low + TWP - TW, jnp.zeros((240, LANES), F32)))
    for b in range(2):
        wide_ref[:, b * LANES : (b + 1) * LANES] = chain(runs[b], line)
    for w in range(NW):
        deep_ref[TWP * w : TWP * w + TW, :] = wide_ref[TW * w : TW * w + TW, :]
    row = lax.broadcasted_iota(jnp.int32, (256, 256), 0)
    column = lanes_of((256, 256))
    codes_here = ((column & 31) == TW) & ((row >> 5) == (column >> 5)) & ((row & 31) < TW)
    full = jnp.where(codes_here, 1.0, deep_ref[...])
    hi = full.astype(BF16)
    hi_ref[...] = hi
    lo_ref[...] = (full - hi.astype(F32)).astype(BF16)
    copies[last].wait()
    copies[0].wait()
    wide_tail_ref[:, 0:TAIL] = tail_ref[...]
    z_ref[last, 0:240, :] = wrapped(z_ref[0, 0:240, :], wide_tail_ref[...], lanes_of((240, LANES)))
    tile_copy.wait()
    line = lanes_of((8, LANES))
    codes = jnp.zeros((8, LANES), F32)
    for j in range(NB):
        tile = tile_ref[0, j]
        there = tile >= 0
        safe = jnp.maximum(tile, 0)
        row = (safe * 4370) >> 16
        col = safe - row * COLS
        row = jnp.where(there, row, 0).astype(F32)
        col = jnp.where(there, col, COLS).astype(F32)
        codes = jnp.where(line == IDX + j, row, codes)
        codes = jnp.where(line == IDX + NB + j, col, codes)
    z_ref[PIECES - 1, 240:248, :] = codes
    conduct_copy.wait()
    lane = lanes_of((1, LANES))
    row_ref[...] = jnp.zeros((8, LANES), F32)
    row_ref[0:1, 0:TAIL] = conduct_ref[pl.ds((PIECES - 1) * LANES, TAIL)].reshape(1, TAIL)
    cut_ref[...] = jnp.zeros((16, LANES), F32)
    for q in range(PIECES):
        if q < PIECES - 1:
            part = conduct_ref[pl.ds(q * LANES, LANES)].reshape(1, LANES)
        else:
            part = wrapped(conduct_ref[pl.ds(0, LANES)].reshape(1, LANES), row_ref[0:1, :], lane)
        hi = part.astype(BF16).astype(F32)
        cut_ref[q : q + 1, :] = hi
        cut_ref[PIECES + q : PIECES + q + 1, :] = part - hi
    for q in range(PIECES):
        if 0 < q < last:
            copies[q].wait()
        for k in range(8):
            out_ref[k, :, q * LANES : (q + 1) * LANES] = z_ref.at[q][pl.ds(k, TWP, stride=8), :].astype(BF16)


def mix_body(x_ref, hi_ref, lo_ref, cut_ref, out_ref, z_ref):
    x = x_ref[...]
    parts = jnp.dot(jnp.concatenate([hi_ref[...], lo_ref[...]], axis=0), x, preferred_element_type=F32)
    mixed = parts[0:256] + parts[256:512]
    m = lax.axis_index("tm")
    for e in range(2):
        part = cut_ref[pl.ds(2 * m + e, 1), :]
        z_ref[pl.ds(PIECES + e, 256, stride=8), :] = jnp.broadcast_to(part, (256, LANES))
    for w in range(NW):
        for q in range(PIECES):
            z_ref[pl.ds(w * 8 + q, TWP, stride=64), :] = mixed[TWP * w : TWP * (w + 1), q * LANES : (q + 1) * LANES]
    out_ref[...] = z_ref[0:2048, :].astype(BF16)


def sweep(load, k_ref, store):
    before, here, conduct = None, load(0), k_ref[0:1, :]
    u = here * conduct
    for s in range(ROWS):
        laplace = turn(u, 1) + turn(u, -1) - 4.0 * u
        if before is not None:
            laplace = laplace + before
        if s + 1 < ROWS:
            after, conduct_after = load(s + 1), k_ref[s + 1 : s + 2, :]
            u_after = after * conduct_after
            laplace = laplace + u_after
        store(s, here + conduct * laplace)
        if s + 1 < ROWS:
            before, here, conduct, u = u, after, conduct_after, u_after


def piece(value, q):
    return value[:, q * LANES : (q + 1) * LANES]


def moved(take, source, target, lane):
    a, first = source // LANES, source % LANES
    cells = take(a)
    if first + TC > LANES:
        cells = jnp.where(lane >= first, cells, take(a + 1))
    return turn(cells, target - source)


def spread_body(x_ref, out_ref, kept_ref, code_ref, z_ref, w_ref, table_ref, slot_ref, sem):
    lane = lanes_of((8, LANES))
    z_ref[0:2048, :] = x_ref[...].astype(F32)
    codes = z_ref[pl.ds(PIECES - 1, ROWS, stride=64), :]
    line = lanes_of((ROWS, LANES))
    codes = jnp.where(line < NB, turn(codes, -IDX - NB) * ROWS + turn(codes, -IDX), 0.0)
    code_ref[...] = jnp.transpose(codes)[0:NB, :].astype(jnp.int32)
    slot_copy = pltpu.make_async_copy(code_ref, slot_ref, sem)
    slot_copy.start()
    for q in range(PIECES):
        hi, lo = q, PIECES + q
        kept_ref[:, q * LANES : (q + 1) * LANES] = (
            z_ref[pl.ds((hi // 2) * 8 + 6 + hi % 2, ROWS, stride=64), :]
            + z_ref[pl.ds((lo // 2) * 8 + 6 + lo % 2, ROWS, stride=64), :]
        )

    def arrived(s):
        return jnp.concatenate([z_ref[pl.ds(s * 64 + q, 8, stride=8), :] for q in range(PIECES)], axis=1)

    def keep(s, value):
        w_ref[s] = value

    def cut(s, value):
        for c in range(COLS):
            table_ref[c * ROWS + s] = moved(lambda a: piece(value, a), c * TC, 0, lane)

    sweep(arrived, kept_ref, keep)
    sweep(lambda s: w_ref[s], kept_ref, keep)
    for s in range(ROWS):
        cut(s, w_ref[s])
    table_ref[BLANK] = jnp.zeros((8, LANES), F32)

    slot_copy.wait()
    ahead = 2
    waiting = {}
    for s in range(ROWS + ahead):
        if s < ROWS:
            waiting[s] = [table_ref[slot_ref[j, s]] for j in range(NB)]
        if s >= ahead:
            tiles = waiting.pop(s - ahead)
            runs = [[], [], []]
            for j in range(NB):
                for _, b, low, high, rotation in span(j * TC, 0):
                    runs[b].append((low, high, turn(tiles[j], rotation)))
            for b in range(3):
                out_ref[s - ahead, :, b * LANES : (b + 1) * LANES] = chain(runs[b], lane).astype(BF16)


def observe_body(x_ref, f_ref, weight_ref, out_ref, x2_ref, g_ref):
    lane = lanes_of((8, LANES))
    runs = {}
    for tau in range(TW):
        value = x_ref[tau].astype(F32)
        for j in range(NB):
            cells = moved(lambda a: piece(value, a), j * TC, tau * TC, lane)
            for _, b, low, high, _ in span(tau * TC, 0):
                runs.setdefault((j, b), []).append((low, high, cells))
        for key in [key for key in runs if (key[1] + 1) * LANES <= (tau + 1) * TC or tau == TW - 1]:
            j, b = key
            x2_ref[j, :, b * LANES : (b + 1) * LANES] = chain(runs.pop(key), lane)
    total = jnp.zeros((8, 64), F32)
    for j in range(NB):
        total = total + lax.dot_general(
            x2_ref[j, :, 0 : TW * TC].astype(BF16),
            f_ref[j],
            (((1,), (1,)), ((), ())),
            preferred_element_type=F32,
        )
    weighted = (weight_ref[...] * total).astype(BF16)
    for j in range(NB):
        g_ref[j, :, 0 : TW * TC] = jnp.dot(weighted, f_ref[j], preferred_element_type=F32)
    for tau in range(TW):
        runs = [[], [], []]
        for j in range(NB):
            cells = moved(lambda a: g_ref[j, :, a * LANES : (a + 1) * LANES], tau * TC, j * TC, lane)
            for _, b, low, high, _ in span(j * TC, 0):
                runs[b].append((low, high, cells))
        for b in range(3):
            out_ref[tau, :, b * LANES : (b + 1) * LANES] = chain(runs[b], lane).astype(BF16)
    out_ref[TW:TWP] = jnp.zeros((TWP - TW, 8, NB * TC), BF16)


def collect_body(slot_any, x_ref, k_ref, out_ref, z_ref, w_ref, table_ref, slot_ref, sem):
    slot_copy = pltpu.make_async_copy(slot_any, slot_ref, sem)
    slot_copy.start()
    lane = lanes_of((8, LANES))
    table_ref[...] = jnp.zeros(table_ref.shape, F32)
    slot_copy.wait()

    def reader(s, carry):
        value = x_ref[s].astype(F32)
        tiles = [slot_ref[j, s] for j in range(NB)]
        sums = []
        for j in range(NB):
            sums.append(table_ref[tiles[j]] + moved(lambda a: piece(value, a), j * TC, 0, lane))
        for j in range(NB):
            table_ref[tiles[j]] = sums[j]
        return carry

    lax.fori_loop(0, ROWS, reader, 0, unroll=True)

    def joined(s):
        runs = [[] for _ in range(PIECES)]
        for c in range(COLS):
            tile = table_ref[c * ROWS + s]
            for _, b, low, high, rotation in span(c * TC, 0):
                runs[b].append((low, high, turn(tile, rotation)))
        runs[-1].append((TAIL, TAIL + 2, turn(table_ref[s], TAIL)))
        runs[-1].append((TAIL + 2, LANES - 2, jnp.zeros((8, LANES), F32)))
        runs[-1].append((LANES - 2, LANES, turn(table_ref[(COLS - 1) * ROWS + s], TAIL)))
        return jnp.concatenate([chain(run, lane) for run in runs], axis=1)

    def keep(s, value):
        w_ref[s] = value

    def leave(s, value):
        for q in range(PIECES):
            z_ref[pl.ds(s * 8 * PIECES + q, 8, stride=PIECES), :] = piece(value, q)

    for s in range(ROWS):
        keep(s, joined(s))
    for _ in range(DIFF):
        sweep(lambda s: w_ref[s], k_ref, keep)
    for s in range(ROWS):
        leave(s, w_ref[s])
    out_ref[...] = z_ref[0:1536, :].astype(BF16)


def unmix_body(x_ref, hi_ref, lo_ref, out_ref, z_ref, w_ref):
    z_ref[0:1536, :] = x_ref[...].astype(F32)
    for w in range(NW):
        for q in range(PIECES):
            w_ref[TWP * w : TWP * (w + 1), q * LANES : (q + 1) * LANES] = z_ref[
                pl.ds(w * PIECES + q, TWP, stride=NW * PIECES), :
            ].astype(BF16)
    x = w_ref[...]
    down = (((0,), (0,)), ((), ()))
    mixed = lax.dot_general(hi_ref[...], x, down, preferred_element_type=F32) + lax.dot_general(
        lo_ref[...], x, down, preferred_element_type=F32
    )
    out_ref[...] = mixed.astype(BF16)


def image_body(x_ref, d_ref, r_ref, image_ref, sums_ref, z_ref):
    for q in range(PIECES):
        z_ref[q, 0:256, :] = x_ref[:, q * LANES : (q + 1) * LANES].astype(F32)
    totals = [jnp.zeros((8, 1), F32) for _ in range(4)]
    for q in range(PIECES):
        width = TAIL if q == PIECES - 1 else LANES
        at = pl.ds(q * LANES, width)
        sums = [jnp.zeros((8, width), F32) for _ in range(4)]
        for t in range(TW):
            d = d_ref[t, :, at]
            r = r_ref[t, :, at]
            image = d + z_ref.at[q][pl.ds(t, 8, stride=TWP), :][:, 0:width]
            image_ref[t, :, at] = image
            for i, (left, right) in enumerate(((r, r), (d, image), (r, image), (image, image))):
                sums[i] = sums[i] + left * right
        for i in range(4):
            totals[i] = totals[i] + jnp.sum(sums[i], axis=1, keepdims=True)
    lane = lanes_of((8, LANES))
    k = lax.broadcasted_iota(jnp.int32, (8, LANES), 0)
    spread = jnp.zeros((8, LANES), F32)
    for i in range(4):
        spread = jnp.where(lane == k * 4 + i, totals[i], spread)
    line = jnp.sum(spread, axis=0, keepdims=True)
    sums_ref[...] = jnp.broadcast_to(line, sums_ref.shape)


def update_body(sums_ref, it_ref, r_ref, d_ref, image_ref, it_out, r_out, d_out, it_new, r_new, d_new, sem):
    line = jnp.sum(sums_ref[...], axis=0, keepdims=True)
    lane = lanes_of((8, LANES))
    k = lax.broadcasted_iota(jnp.int32, (8, LANES), 0)
    rr, dq, rq, qq = [
        jnp.sum(jnp.where(lane == k * 4 + i, line, 0.0), axis=1, keepdims=True) for i in range(4)
    ]
    step = rr / dq
    norm = jnp.maximum(rr + step * (step * qq - 2.0 * rq), 0.0)
    ratio = norm / rr
    count = 3
    rows = TW // count
    copies = []
    for i in range(count):
        for t in range(i * rows, (i + 1) * rows):
            d = d_ref[t]
            after = r_ref[t] - step * image_ref[t]
            it_new[t] = it_ref[t] + step * d
            r_new[t] = after
            d_new[t] = after + ratio * d
        at = pl.ds(i * rows, rows)
        for n, (new, out) in enumerate(((it_new, it_out), (r_new, r_out), (d_new, d_out))):
            copies.append(pltpu.make_async_copy(new.at[at], out.at[at], sem.at[n, i]))
            copies[-1].start()
    for copy in copies:
        copy.wait()


def shape(dims, dtype):
    return jax.ShapeDtypeStruct(dims, dtype)


def local(
    iterate, residual, direction, diffusivity, temporal_factor, block_tile, footprints, obs_weight
):
    both = ("space", "tm")
    iterate, residual, direction = [
        jnp.transpose(value, (1, 0, 2)) for value in (iterate, residual, direction)
    ]
    grid = (ROWS, 8, WIDE)
    with jax.named_scope("prepare"):
        message, hi, lo, cut = call(
            prepare_body,
            (
                shape((8, TWP, WIDE), BF16),
                shape((256, 256), BF16),
                shape((256, 256), BF16),
                shape((16, LANES), F32),
            ),
            [
                pltpu.VMEM((PIECES, 264, LANES), F32),
                pltpu.VMEM((240, TAIL), F32),
                pltpu.VMEM((240, LANES), F32),
                pltpu.SMEM((1, NB), jnp.int32),
                pltpu.VMEM((240, 240), F32),
                pltpu.VMEM((240, 256), F32),
                pltpu.VMEM((256, 256), F32),
                pltpu.VMEM((LON,), F32),
                pltpu.VMEM((8, LANES), F32),
                pltpu.SemaphoreType.DMA((6,)),
                pltpu.SemaphoreType.DMA((3,)),
            ],
            "hhhh",
        )(
            *[
                pltpu.with_memory_space_constraint(value, pltpu.HBM)
                for value in (block_tile, direction.reshape(240, LON), temporal_factor, diffusivity)
            ]
        )
        message = lax.all_to_all(message, "tm", 0, 0, tiled=True)
    with jax.named_scope("mix"):
        message = call(mix_body, shape((2048, LANES), BF16), [pltpu.VMEM((2112, LANES), F32)])(
            message.reshape(256, WIDE), hi, lo, cut
        )
        message = lax.all_to_all(message.reshape(256, 8, LANES), both, 0, 0, tiled=True)
    with jax.named_scope("spread"):
        message, conduct, slots = call(
            spread_body,
            (shape((ROWS, 8, NB * TC), BF16), shape((ROWS, WIDE), F32), shape((NB, ROWS), jnp.int32)),
            [
                pltpu.VMEM((2112, LANES), F32),
                pltpu.VMEM(grid, F32),
                pltpu.VMEM((BLANK + 1, 8, LANES), F32),
                pltpu.SMEM((NB, ROWS), jnp.int32),
                pltpu.SemaphoreType.DMA,
            ],
        )(message.reshape(2048, LANES))
        message = lax.all_to_all(message, "space", 0, 0, tiled=True)
    with jax.named_scope("observe"):
        message = call(
            observe_body,
            shape((TWP, 8, NB * TC), BF16),
            [pltpu.VMEM((NB, 8, 1536), F32), pltpu.VMEM((NB, 8, 1536), F32)],
        )(message, footprints[0], obs_weight[0])
        message = lax.all_to_all(message, "space", 0, 0, tiled=True)
    with jax.named_scope("collect"):
        message = call(
            collect_body,
            shape((1536, LANES), BF16),
            [
                pltpu.VMEM((1584, LANES), F32),
                pltpu.VMEM(grid, F32),
                pltpu.VMEM((BLANK + 1, 8, LANES), F32),
                pltpu.SMEM((NB, ROWS), jnp.int32),
                pltpu.SemaphoreType.DMA,
            ],
            "h",
        )(slots, message, conduct)
        message = lax.all_to_all(message.reshape(768, 2, LANES), both, 0, 0, tiled=True)
    with jax.named_scope("unmix"):
        message = call(
            unmix_body,
            shape((256, WIDE), BF16),
            [pltpu.VMEM((1584, LANES), F32), pltpu.VMEM((256, WIDE), BF16)],
        )(message.reshape(1536, LANES), hi, lo)
        message = lax.all_to_all(message.reshape(8, TWP, WIDE), "tm", 0, 0, tiled=True)
    with jax.named_scope("image"):
        image, sums = call(
            image_body,
            (shape((TW, 8, LON), F32), shape((256, LANES), F32)),
            [pltpu.VMEM((PIECES, 288, LANES), F32)],
        )(message.reshape(256, WIDE), direction, residual)
        sums = lax.all_to_all(sums, both, 0, 0, tiled=True)
    with jax.named_scope("update"):
        whole = (TW, 8, LON)
        outs = call(
            update_body,
            tuple(shape(whole, F32) for _ in range(3)),
            [pltpu.VMEM(whole, F32) for _ in range(3)] + [pltpu.SemaphoreType.DMA((3, 3))],
            out_places="hhh",
        )(sums, iterate, residual, direction, image)
    return tuple(jnp.transpose(value, (1, 0, 2)) for value in outs)


def solution(mesh):
    return jax.shard_map(
        local,
        mesh=mesh,
        in_specs=(
            P(None, "tm", "space"),
            P(None, "tm", "space"),
            P(None, "tm", "space"),
            P("space"),
            P(),
            P("tm", "space"),
            P("tm", "space", None, None),
            P("tm", "space", None),
        ),
        out_specs=(P(None, "tm", "space"), P(None, "tm", "space"), P(None, "tm", "space")),
        check_vma=False,
    )
```

```python
import jax
import jax.numpy as jnp
from jax import lax
from jax.experimental import pallas as pl
from jax.experimental.pallas import tpu as pltpu
from jax.sharding import PartitionSpec as P

LON = 720
TC = 48
NB = 8
DIFF = 2
LANES = 128
WIDE = 768
PIECES = WIDE // LANES
ROWS = 32
TW = 30
TWP = 32
NW = 8
COLS = LON // TC
BLANK = COLS * ROWS
TAIL = LON - (PIECES - 1) * LANES
IDX = 82
F32 = jnp.float32
BF16 = jnp.bfloat16


def call(body, outs, scratch=(), places="", out_places=None):
    space = {"v": pltpu.VMEM, "s": pltpu.SMEM, "h": pltpu.HBM}

    def run(*args):
        kinds = places + "v" * (len(args) - len(places))
        more = {}
        if out_places is not None:
            more["out_specs"] = tuple(pl.BlockSpec(memory_space=space[kind]) for kind in out_places)
        return pl.pallas_call(
            body,
            out_shape=outs,
            in_specs=[pl.BlockSpec(memory_space=space[kind]) for kind in kinds],
            scratch_shapes=list(scratch),
            compiler_params=pltpu.CompilerParams(vmem_limit_bytes=40 * 1024 * 1024),
            **more,
        )(*args)

    return run


def lanes_of(shape):
    return lax.broadcasted_iota(jnp.int32, shape, len(shape) - 1)


def turn(value, shift):
    shift = shift % value.shape[-1]
    return value if shift == 0 else pltpu.roll(value, shift, value.ndim - 1)


def span(start, source, length=TC):
    parts = []
    done = 0
    while done < length:
        a, b = (source + done) // LANES, (start + done) // LANES
        take = min(length - done, (a + 1) * LANES - source - done, (b + 1) * LANES - start - done)
        low = start + done - b * LANES
        parts.append((a, b, low, low + take, (start - source) % LANES))
        done += take
    return parts


def chain(parts, lane, below=None):
    parts = sorted(parts, key=lambda part: part[0])
    result = parts[-1][2]
    for low, high, value in reversed(parts[:-1]):
        result = jnp.where(lane < high, value, result)
    return result


def wrapped(first, tail, lane):
    return jnp.where(
        lane < TAIL,
        tail,
        jnp.where(lane < TAIL + 2, turn(first, TAIL), jnp.where(lane >= LANES - 2, turn(tail, TC), 0.0)),
    )


def prepare_body(
    tile_hbm, d_hbm, factor_hbm, conduct_hbm, out_ref, hi_ref, lo_ref, cut_ref,
    z_ref, tail_ref, wide_tail_ref, tile_ref, factor_ref, wide_ref, deep_ref, conduct_ref, row_ref, sem, more_sem,
):
    factor_copy = pltpu.make_async_copy(factor_hbm, factor_ref, more_sem.at[0])
    tile_copy = pltpu.make_async_copy(tile_hbm, tile_ref, more_sem.at[1])
    conduct_copy = pltpu.make_async_copy(conduct_hbm, conduct_ref, more_sem.at[2])
    last = PIECES - 1
    copies = [
        pltpu.make_async_copy(
            d_hbm.at[:, pl.ds(q * LANES, LANES)], z_ref.at[q, pl.ds(0, 240), :], sem.at[q]
        )
        for q in range(last)
    ] + [pltpu.make_async_copy(d_hbm.at[:, pl.ds(last * LANES, TAIL)], tail_ref, sem.at[last])]
    factor_copy.start()
    for copy in copies:
        copy.start()
    tile_copy.start()
    conduct_copy.start()
    for q in range(PIECES - 1):
        z_ref[q, 240:256, :] = jnp.zeros((16, LANES), F32)
    z_ref[PIECES - 1, 248:256, :] = jnp.zeros((8, LANES), F32)
    deep_ref[...] = jnp.zeros((256, 256), F32)
    wide_ref[:, LANES:] = jnp.zeros((240, LANES), F32)
    factor_copy.wait()
    wide_ref[:, 0:240] = factor_ref[...]
    factor = wide_ref[...]
    line = lanes_of((240, LANES))
    runs = [[], []]
    for w in range(NW):
        for a, b, low, high, rotation in span(TWP * w, TW * w, TW):
            runs[b].append((low, high, turn(piece(factor, a), rotation)))
        low = TWP * w % LANES + TW
        runs[TWP * w // LANES].append((low, low + TWP - TW, jnp.zeros((240, LANES), F32)))
    for b in range(2):
        wide_ref[:, b * LANES : (b + 1) * LANES] = chain(runs[b], line)
    for w in range(NW):
        deep_ref[TWP * w : TWP * w + TW, :] = wide_ref[TW * w : TW * w + TW, :]
    row = lax.broadcasted_iota(jnp.int32, (256, 256), 0)
    column = lanes_of((256, 256))
    codes_here = ((column & 31) == TW) & ((row >> 5) == (column >> 5)) & ((row & 31) < TW)
    full = jnp.where(codes_here, 1.0, deep_ref[...])
    hi = full.astype(BF16)
    hi_ref[...] = hi
    lo_ref[...] = (full - hi.astype(F32)).astype(BF16)
    copies[last].wait()
    copies[0].wait()
    wide_tail_ref[:, 0:TAIL] = tail_ref[...]
    z_ref[last, 0:240, :] = wrapped(z_ref[0, 0:240, :], wide_tail_ref[...], lanes_of((240, LANES)))
    tile_copy.wait()
    line = lanes_of((8, LANES))
    codes = jnp.zeros((8, LANES), F32)
    for j in range(NB):
        tile = tile_ref[0, j]
        there = tile >= 0
        safe = jnp.maximum(tile, 0)
        row = (safe * 4370) >> 16
        col = safe - row * COLS
        row = jnp.where(there, row, 0).astype(F32)
        col = jnp.where(there, col, COLS).astype(F32)
        codes = jnp.where(line == IDX + j, row, codes)
        codes = jnp.where(line == IDX + NB + j, col, codes)
    z_ref[PIECES - 1, 240:248, :] = codes
    conduct_copy.wait()
    lane = lanes_of((1, LANES))
    row_ref[...] = jnp.zeros((8, LANES), F32)
    row_ref[0:1, 0:TAIL] = conduct_ref[pl.ds((PIECES - 1) * LANES, TAIL)].reshape(1, TAIL)
    cut_ref[...] = jnp.zeros((16, LANES), F32)
    for q in range(PIECES):
        if q < PIECES - 1:
            part = conduct_ref[pl.ds(q * LANES, LANES)].reshape(1, LANES)
        else:
            part = wrapped(conduct_ref[pl.ds(0, LANES)].reshape(1, LANES), row_ref[0:1, :], lane)
        hi = part.astype(BF16).astype(F32)
        cut_ref[q : q + 1, :] = hi
        cut_ref[PIECES + q : PIECES + q + 1, :] = part - hi
    for q in range(PIECES):
        if 0 < q < last:
            copies[q].wait()
        for k in range(8):
            out_ref[k, :, q * LANES : (q + 1) * LANES] = z_ref.at[q][pl.ds(k, TWP, stride=8), :].astype(BF16)


def mix_body(x_ref, hi_ref, lo_ref, cut_ref, out_ref, z_ref):
    x = x_ref[...]
    parts = jnp.dot(jnp.concatenate([hi_ref[...], lo_ref[...]], axis=0), x, preferred_element_type=F32)
    mixed = parts[0:256] + parts[256:512]
    m = lax.axis_index("tm")
    for e in range(2):
        part = cut_ref[pl.ds(2 * m + e, 1), :]
        z_ref[pl.ds(PIECES + e, 256, stride=8), :] = jnp.broadcast_to(part, (256, LANES))
    for w in range(NW):
        for q in range(PIECES):
            z_ref[pl.ds(w * 8 + q, TWP, stride=64), :] = mixed[TWP * w : TWP * (w + 1), q * LANES : (q + 1) * LANES]
    out_ref[...] = z_ref[0:2048, :].astype(BF16)


def sweep(load, k_ref, store):
    before, here, conduct = None, load(0), k_ref[0:1, :]
    u = here * conduct
    for s in range(ROWS):
        laplace = turn(u, 1) + turn(u, -1) - 4.0 * u
        if before is not None:
            laplace = laplace + before
        if s + 1 < ROWS:
            after, conduct_after = load(s + 1), k_ref[s + 1 : s + 2, :]
            u_after = after * conduct_after
            laplace = laplace + u_after
        store(s, here + conduct * laplace)
        if s + 1 < ROWS:
            before, here, conduct, u = u, after, conduct_after, u_after


def piece(value, q):
    return value[:, q * LANES : (q + 1) * LANES]


def moved(take, source, target, lane):
    a, first = source // LANES, source % LANES
    cells = take(a)
    if first + TC > LANES:
        cells = jnp.where(lane >= first, cells, take(a + 1))
    return turn(cells, target - source)


def spread_body(x_ref, out_ref, kept_ref, code_ref, z_ref, w_ref, table_ref, slot_ref, sem):
    lane = lanes_of((8, LANES))
    z_ref[0:2048, :] = x_ref[...].astype(F32)
    codes = z_ref[pl.ds(PIECES - 1, ROWS, stride=64), :]
    line = lanes_of((ROWS, LANES))
    codes = jnp.where(line < NB, turn(codes, -IDX - NB) * ROWS + turn(codes, -IDX), 0.0)
    code_ref[...] = jnp.transpose(codes)[0:NB, :].astype(jnp.int32)
    slot_copy = pltpu.make_async_copy(code_ref, slot_ref, sem)
    slot_copy.start()
    for q in range(PIECES):
        hi, lo = q, PIECES + q
        kept_ref[:, q * LANES : (q + 1) * LANES] = (
            z_ref[pl.ds((hi // 2) * 8 + 6 + hi % 2, ROWS, stride=64), :]
            + z_ref[pl.ds((lo // 2) * 8 + 6 + lo % 2, ROWS, stride=64), :]
        )

    def arrived(s):
        return jnp.concatenate([z_ref[pl.ds(s * 64 + q, 8, stride=8), :] for q in range(PIECES)], axis=1)

    def keep(s, value):
        w_ref[s] = value

    def cut(s, value):
        for c in range(COLS):
            table_ref[c * ROWS + s] = moved(lambda a: piece(value, a), c * TC, 0, lane)

    sweep(arrived, kept_ref, keep)
    sweep(lambda s: w_ref[s], kept_ref, keep)
    for s in range(ROWS):
        cut(s, w_ref[s])
    table_ref[BLANK] = jnp.zeros((8, LANES), F32)

    slot_copy.wait()
    ahead = 2
    waiting = {}
    for s in range(ROWS + ahead):
        if s < ROWS:
            waiting[s] = [table_ref[slot_ref[j, s]] for j in range(NB)]
        if s >= ahead:
            tiles = waiting.pop(s - ahead)
            runs = [[], [], []]
            for j in range(NB):
                for _, b, low, high, rotation in span(j * TC, 0):
                    runs[b].append((low, high, turn(tiles[j], rotation)))
            for b in range(3):
                out_ref[s - ahead, :, b * LANES : (b + 1) * LANES] = chain(runs[b], lane).astype(BF16)


def observe_body(x_ref, f_ref, weight_ref, out_ref, x2_ref, g_ref):
    lane = lanes_of((8, LANES))
    runs = {}
    for tau in range(TW):
        value = x_ref[tau].astype(F32)
        for j in range(NB):
            cells = moved(lambda a: piece(value, a), j * TC, tau * TC, lane)
            for _, b, low, high, _ in span(tau * TC, 0):
                runs.setdefault((j, b), []).append((low, high, cells))
        for key in [key for key in runs if (key[1] + 1) * LANES <= (tau + 1) * TC or tau == TW - 1]:
            j, b = key
            x2_ref[j, :, b * LANES : (b + 1) * LANES] = chain(runs.pop(key), lane)
    total = jnp.zeros((8, 64), F32)
    for j in range(NB):
        total = total + lax.dot_general(
            x2_ref[j, :, 0 : TW * TC].astype(BF16),
            f_ref[j],
            (((1,), (1,)), ((), ())),
            preferred_element_type=F32,
        )
    weighted = (weight_ref[...] * total).astype(BF16)
    for j in range(NB):
        g_ref[j, :, 0 : TW * TC] = jnp.dot(weighted, f_ref[j], preferred_element_type=F32)
    for tau in range(TW):
        runs = [[], [], []]
        for j in range(NB):
            cells = moved(lambda a: g_ref[j, :, a * LANES : (a + 1) * LANES], tau * TC, j * TC, lane)
            for _, b, low, high, _ in span(j * TC, 0):
                runs[b].append((low, high, cells))
        for b in range(3):
            out_ref[tau, :, b * LANES : (b + 1) * LANES] = chain(runs[b], lane).astype(BF16)
    out_ref[TW:TWP] = jnp.zeros((TWP - TW, 8, NB * TC), BF16)


def collect_body(slot_any, x_ref, k_ref, out_ref, z_ref, w_ref, table_ref, pieces_ref, slot_ref, sem):
    slot_copy = pltpu.make_async_copy(slot_any, slot_ref, sem)
    slot_copy.start()
    lane = lanes_of((8, LANES))
    table_ref[...] = jnp.zeros(table_ref.shape, F32)
    for s in range(ROWS):
        value = x_ref[s].astype(F32)
        for j in range(NB):
            pieces_ref[s * NB + j] = moved(lambda a: piece(value, a), j * TC, 0, lane)
    slot_copy.wait()

    def reader(s, carry):
        tiles = [slot_ref[j, s] for j in range(NB)]
        sums = []
        for j in range(NB):
            sums.append(table_ref[tiles[j]] + pieces_ref[s * NB + j])
        for j in range(NB):
            table_ref[tiles[j]] = sums[j]
        return carry

    lax.fori_loop(0, ROWS, reader, 0, unroll=True)

    def joined(s):
        runs = [[] for _ in range(PIECES)]
        for c in range(COLS):
            tile = table_ref[c * ROWS + s]
            for _, b, low, high, rotation in span(c * TC, 0):
                runs[b].append((low, high, turn(tile, rotation)))
        runs[-1].append((TAIL, TAIL + 2, turn(table_ref[s], TAIL)))
        runs[-1].append((TAIL + 2, LANES - 2, jnp.zeros((8, LANES), F32)))
        runs[-1].append((LANES - 2, LANES, turn(table_ref[(COLS - 1) * ROWS + s], TAIL)))
        return jnp.concatenate([chain(run, lane) for run in runs], axis=1)

    def keep(s, value):
        w_ref[s] = value

    def leave(s, value):
        for q in range(PIECES):
            z_ref[pl.ds(s * 8 * PIECES + q, 8, stride=PIECES), :] = piece(value, q)

    for s in range(ROWS):
        keep(s, joined(s))
    for _ in range(DIFF):
        sweep(lambda s: w_ref[s], k_ref, keep)
    for s in range(ROWS):
        leave(s, w_ref[s])
    out_ref[...] = z_ref[0:1536, :].astype(BF16)


def unmix_body(x_ref, hi_ref, lo_ref, out_ref, z_ref, w_ref):
    z_ref[0:1536, :] = x_ref[...].astype(F32)
    for w in range(NW):
        for q in range(PIECES):
            w_ref[TWP * w : TWP * (w + 1), q * LANES : (q + 1) * LANES] = z_ref[
                pl.ds(w * PIECES + q, TWP, stride=NW * PIECES), :
            ].astype(BF16)
    x = w_ref[...]
    down = (((0,), (0,)), ((), ()))
    mixed = lax.dot_general(hi_ref[...], x, down, preferred_element_type=F32) + lax.dot_general(
        lo_ref[...], x, down, preferred_element_type=F32
    )
    out_ref[...] = mixed.astype(BF16)


def image_body(x_ref, d_ref, r_ref, image_ref, sums_ref, z_ref):
    for q in range(PIECES):
        z_ref[q, 0:256, :] = x_ref[:, q * LANES : (q + 1) * LANES].astype(F32)
    totals = [jnp.zeros((8, 1), F32) for _ in range(4)]
    for q in range(PIECES):
        width = TAIL if q == PIECES - 1 else LANES
        at = pl.ds(q * LANES, width)
        sums = [jnp.zeros((8, width), F32) for _ in range(4)]
        for t in range(TW):
            d = d_ref[t, :, at]
            r = r_ref[t, :, at]
            image = d + z_ref.at[q][pl.ds(t, 8, stride=TWP), :][:, 0:width]
            image_ref[t, :, at] = image
            for i, (left, right) in enumerate(((r, r), (d, image), (r, image), (image, image))):
                sums[i] = sums[i] + left * right
        for i in range(4):
            totals[i] = totals[i] + jnp.sum(sums[i], axis=1, keepdims=True)
    lane = lanes_of((8, LANES))
    k = lax.broadcasted_iota(jnp.int32, (8, LANES), 0)
    spread = jnp.zeros((8, LANES), F32)
    for i in range(4):
        spread = jnp.where(lane == k * 4 + i, totals[i], spread)
    line = jnp.sum(spread, axis=0, keepdims=True)
    sums_ref[...] = jnp.broadcast_to(line, sums_ref.shape)


def update_body(sums_ref, it_ref, r_ref, d_ref, image_ref, it_out, r_out, d_out, it_new, r_new, d_new, sem):
    line = jnp.sum(sums_ref[...], axis=0, keepdims=True)
    lane = lanes_of((8, LANES))
    k = lax.broadcasted_iota(jnp.int32, (8, LANES), 0)
    rr, dq, rq, qq = [
        jnp.sum(jnp.where(lane == k * 4 + i, line, 0.0), axis=1, keepdims=True) for i in range(4)
    ]
    step = rr / dq
    norm = jnp.maximum(rr + step * (step * qq - 2.0 * rq), 0.0)
    ratio = norm / rr
    copies = []
    for i, (start, stop) in enumerate(((0, 3), (3, 12), (12, 21), (21, TW))):
        for t in range(start, stop):
            d = d_ref[t]
            after = r_ref[t] - step * image_ref[t]
            it_new[t] = it_ref[t] + step * d
            r_new[t] = after
            d_new[t] = after + ratio * d
        at = pl.ds(start, stop - start)
        for n, (new, out) in enumerate(((it_new, it_out), (r_new, r_out), (d_new, d_out))):
            copies.append(pltpu.make_async_copy(new.at[at], out.at[at], sem.at[n, i]))
            copies[-1].start()
    for copy in copies:
        copy.wait()


def shape(dims, dtype):
    return jax.ShapeDtypeStruct(dims, dtype)


def local(
    iterate, residual, direction, diffusivity, temporal_factor, block_tile, footprints, obs_weight
):
    both = ("space", "tm")
    iterate, residual, direction = [
        jnp.transpose(value, (1, 0, 2)) for value in (iterate, residual, direction)
    ]
    grid = (ROWS, 8, WIDE)
    with jax.named_scope("prepare"):
        message, hi, lo, cut = call(
            prepare_body,
            (
                shape((8, TWP, WIDE), BF16),
                shape((256, 256), BF16),
                shape((256, 256), BF16),
                shape((16, LANES), F32),
            ),
            [
                pltpu.VMEM((PIECES, 264, LANES), F32),
                pltpu.VMEM((240, TAIL), F32),
                pltpu.VMEM((240, LANES), F32),
                pltpu.SMEM((1, NB), jnp.int32),
                pltpu.VMEM((240, 240), F32),
                pltpu.VMEM((240, 256), F32),
                pltpu.VMEM((256, 256), F32),
                pltpu.VMEM((LON,), F32),
                pltpu.VMEM((8, LANES), F32),
                pltpu.SemaphoreType.DMA((6,)),
                pltpu.SemaphoreType.DMA((3,)),
            ],
            "hhhh",
        )(
            *[
                pltpu.with_memory_space_constraint(value, pltpu.HBM)
                for value in (block_tile, direction.reshape(240, LON), temporal_factor, diffusivity)
            ]
        )
        message = lax.all_to_all(message, "tm", 0, 0, tiled=True)
    with jax.named_scope("mix"):
        message = call(mix_body, shape((2048, LANES), BF16), [pltpu.VMEM((2112, LANES), F32)])(
            message.reshape(256, WIDE), hi, lo, cut
        )
        message = lax.all_to_all(message.reshape(256, 8, LANES), both, 0, 0, tiled=True)
    with jax.named_scope("spread"):
        message, conduct, slots = call(
            spread_body,
            (shape((ROWS, 8, NB * TC), BF16), shape((ROWS, WIDE), F32), shape((NB, ROWS), jnp.int32)),
            [
                pltpu.VMEM((2112, LANES), F32),
                pltpu.VMEM(grid, F32),
                pltpu.VMEM((BLANK + 1, 8, LANES), F32),
                pltpu.SMEM((NB, ROWS), jnp.int32),
                pltpu.SemaphoreType.DMA,
            ],
        )(message.reshape(2048, LANES))
        message = lax.all_to_all(message, "space", 0, 0, tiled=True)
    with jax.named_scope("observe"):
        message = call(
            observe_body,
            shape((TWP, 8, NB * TC), BF16),
            [pltpu.VMEM((NB, 8, 1536), F32), pltpu.VMEM((NB, 8, 1536), F32)],
        )(message, footprints[0], obs_weight[0])
        message = lax.all_to_all(message, "space", 0, 0, tiled=True)
    with jax.named_scope("collect"):
        message = call(
            collect_body,
            shape((1536, LANES), BF16),
            [
                pltpu.VMEM((1584, LANES), F32),
                pltpu.VMEM(grid, F32),
                pltpu.VMEM((BLANK + 1, 8, LANES), F32),
                pltpu.VMEM((ROWS * NB, 8, LANES), F32),
                pltpu.SMEM((NB, ROWS), jnp.int32),
                pltpu.SemaphoreType.DMA,
            ],
            "h",
        )(slots, message, conduct)
        message = lax.all_to_all(message.reshape(768, 2, LANES), both, 0, 0, tiled=True)
    with jax.named_scope("unmix"):
        message = call(
            unmix_body,
            shape((256, WIDE), BF16),
            [pltpu.VMEM((1584, LANES), F32), pltpu.VMEM((256, WIDE), BF16)],
        )(message.reshape(1536, LANES), hi, lo)
        message = lax.all_to_all(message.reshape(8, TWP, WIDE), "tm", 0, 0, tiled=True)
    with jax.named_scope("image"):
        image, sums = call(
            image_body,
            (shape((TW, 8, LON), F32), shape((256, LANES), F32)),
            [pltpu.VMEM((PIECES, 288, LANES), F32)],
        )(message.reshape(256, WIDE), direction, residual)
        sums = lax.all_to_all(sums, both, 0, 0, tiled=True)
    with jax.named_scope("update"):
        whole = (TW, 8, LON)
        outs = call(
            update_body,
            tuple(shape(whole, F32) for _ in range(3)),
            [pltpu.VMEM(whole, F32) for _ in range(3)] + [pltpu.SemaphoreType.DMA((3, 4))],
            out_places="hhh",
        )(sums, iterate, residual, direction, image)
    return tuple(jnp.transpose(value, (1, 0, 2)) for value in outs)


def solution(mesh):
    return jax.shard_map(
        local,
        mesh=mesh,
        in_specs=(
            P(None, "tm", "space"),
            P(None, "tm", "space"),
            P(None, "tm", "space"),
            P("space"),
            P(),
            P("tm", "space"),
            P("tm", "space", None, None),
            P("tm", "space", None),
        ),
        out_specs=(P(None, "tm", "space"), P(None, "tm", "space"), P(None, "tm", "space")),
        check_vma=False,
    )
```

```python
import jax
import jax.numpy as jnp
from jax import lax
from jax.experimental import pallas as pl
from jax.experimental.pallas import tpu as pltpu
from jax.sharding import PartitionSpec as P

LON = 720
TC = 48
NB = 8
DIFF = 2
LANES = 128
WIDE = 768
PIECES = WIDE // LANES
ROWS = 32
TW = 30
TWP = 32
NW = 8
COLS = LON // TC
BLANK = COLS * ROWS
TAIL = LON - (PIECES - 1) * LANES
IDX = 82
F32 = jnp.float32
BF16 = jnp.bfloat16


def call(body, outs, scratch=(), places="", out_places=None):
    space = {"v": pltpu.VMEM, "s": pltpu.SMEM, "h": pltpu.HBM}

    def run(*args):
        kinds = places + "v" * (len(args) - len(places))
        more = {}
        if out_places is not None:
            more["out_specs"] = tuple(pl.BlockSpec(memory_space=space[kind]) for kind in out_places)
        return pl.pallas_call(
            body,
            out_shape=outs,
            in_specs=[pl.BlockSpec(memory_space=space[kind]) for kind in kinds],
            scratch_shapes=list(scratch),
            compiler_params=pltpu.CompilerParams(vmem_limit_bytes=40 * 1024 * 1024),
            **more,
        )(*args)

    return run


def lanes_of(shape):
    return lax.broadcasted_iota(jnp.int32, shape, len(shape) - 1)


def turn(value, shift):
    shift = shift % value.shape[-1]
    return value if shift == 0 else pltpu.roll(value, shift, value.ndim - 1)


def span(start, source, length=TC):
    parts = []
    done = 0
    while done < length:
        a, b = (source + done) // LANES, (start + done) // LANES
        take = min(length - done, (a + 1) * LANES - source - done, (b + 1) * LANES - start - done)
        low = start + done - b * LANES
        parts.append((a, b, low, low + take, (start - source) % LANES))
        done += take
    return parts


def chain(parts, lane, below=None):
    parts = sorted(parts, key=lambda part: part[0])
    result = parts[-1][2]
    for low, high, value in reversed(parts[:-1]):
        result = jnp.where(lane < high, value, result)
    return result


def wrapped(first, tail, lane):
    return jnp.where(
        lane < TAIL,
        tail,
        jnp.where(lane < TAIL + 2, turn(first, TAIL), jnp.where(lane >= LANES - 2, turn(tail, TC), 0.0)),
    )


def prepare_body(
    tile_hbm, d_hbm, factor_hbm, conduct_hbm, out_ref, hi_ref, lo_ref, cut_ref,
    z_ref, tail_ref, wide_tail_ref, tile_ref, factor_ref, wide_ref, deep_ref, conduct_ref, row_ref, sem, more_sem,
):
    factor_copy = pltpu.make_async_copy(factor_hbm, factor_ref, more_sem.at[0])
    tile_copy = pltpu.make_async_copy(tile_hbm, tile_ref, more_sem.at[1])
    conduct_copy = pltpu.make_async_copy(conduct_hbm, conduct_ref, more_sem.at[2])
    last = PIECES - 1
    copies = [
        pltpu.make_async_copy(
            d_hbm.at[:, pl.ds(q * LANES, LANES)], z_ref.at[q, pl.ds(0, 240), :], sem.at[q]
        )
        for q in range(last)
    ] + [pltpu.make_async_copy(d_hbm.at[:, pl.ds(last * LANES, TAIL)], tail_ref, sem.at[last])]
    factor_copy.start()
    for copy in copies:
        copy.start()
    tile_copy.start()
    conduct_copy.start()
    for q in range(PIECES - 1):
        z_ref[q, 240:256, :] = jnp.zeros((16, LANES), F32)
    z_ref[PIECES - 1, 248:256, :] = jnp.zeros((8, LANES), F32)
    deep_ref[...] = jnp.zeros((256, 256), F32)
    wide_ref[:, LANES:] = jnp.zeros((240, LANES), F32)
    factor_copy.wait()
    wide_ref[:, 0:240] = factor_ref[...]
    factor = wide_ref[...]
    line = lanes_of((240, LANES))
    runs = [[], []]
    for w in range(NW):
        for a, b, low, high, rotation in span(TWP * w, TW * w, TW):
            runs[b].append((low, high, turn(piece(factor, a), rotation)))
        low = TWP * w % LANES + TW
        runs[TWP * w // LANES].append((low, low + TWP - TW, jnp.zeros((240, LANES), F32)))
    for b in range(2):
        wide_ref[:, b * LANES : (b + 1) * LANES] = chain(runs[b], line)
    for w in range(NW):
        deep_ref[TWP * w : TWP * w + TW, :] = wide_ref[TW * w : TW * w + TW, :]
    row = lax.broadcasted_iota(jnp.int32, (256, 256), 0)
    column = lanes_of((256, 256))
    codes_here = ((column & 31) == TW) & ((row >> 5) == (column >> 5)) & ((row & 31) < TW)
    full = jnp.where(codes_here, 1.0, deep_ref[...])
    hi = full.astype(BF16)
    hi_ref[...] = hi
    lo_ref[...] = (full - hi.astype(F32)).astype(BF16)
    copies[last].wait()
    copies[0].wait()
    wide_tail_ref[:, 0:TAIL] = tail_ref[...]
    z_ref[last, 0:240, :] = wrapped(z_ref[0, 0:240, :], wide_tail_ref[...], lanes_of((240, LANES)))
    tile_copy.wait()
    line = lanes_of((8, LANES))
    codes = jnp.zeros((8, LANES), F32)
    for j in range(NB):
        tile = tile_ref[0, j]
        there = tile >= 0
        safe = jnp.maximum(tile, 0)
        row = (safe * 4370) >> 16
        col = safe - row * COLS
        row = jnp.where(there, row, 0).astype(F32)
        col = jnp.where(there, col, COLS).astype(F32)
        codes = jnp.where(line == IDX + j, row, codes)
        codes = jnp.where(line == IDX + NB + j, col, codes)
    z_ref[PIECES - 1, 240:248, :] = codes
    conduct_copy.wait()
    lane = lanes_of((1, LANES))
    row_ref[...] = jnp.zeros((8, LANES), F32)
    row_ref[0:1, 0:TAIL] = conduct_ref[pl.ds((PIECES - 1) * LANES, TAIL)].reshape(1, TAIL)
    cut_ref[...] = jnp.zeros((16, LANES), F32)
    for q in range(PIECES):
        if q < PIECES - 1:
            part = conduct_ref[pl.ds(q * LANES, LANES)].reshape(1, LANES)
        else:
            part = wrapped(conduct_ref[pl.ds(0, LANES)].reshape(1, LANES), row_ref[0:1, :], lane)
        hi = part.astype(BF16).astype(F32)
        cut_ref[q : q + 1, :] = hi
        cut_ref[PIECES + q : PIECES + q + 1, :] = part - hi
    for q in range(PIECES):
        if 0 < q < last:
            copies[q].wait()
        for k in range(8):
            out_ref[k, :, q * LANES : (q + 1) * LANES] = z_ref.at[q][pl.ds(k, TWP, stride=8), :].astype(BF16)


def mix_body(x_ref, hi_ref, lo_ref, cut_ref, out_ref, z_ref):
    x = x_ref[...]
    parts = jnp.dot(jnp.concatenate([hi_ref[...], lo_ref[...]], axis=0), x, preferred_element_type=F32)
    mixed = parts[0:256] + parts[256:512]
    m = lax.axis_index("tm")
    for e in range(2):
        part = cut_ref[pl.ds(2 * m + e, 1), :]
        z_ref[pl.ds(PIECES + e, 256, stride=8), :] = jnp.broadcast_to(part, (256, LANES))
    for w in range(NW):
        for q in range(PIECES):
            z_ref[pl.ds(w * 8 + q, TWP, stride=64), :] = mixed[TWP * w : TWP * (w + 1), q * LANES : (q + 1) * LANES]
    out_ref[...] = z_ref[0:2048, :].astype(BF16)


def sweep(load, k_ref, store):
    before, here, conduct = None, load(0), k_ref[0:1, :]
    u = here * conduct
    for s in range(ROWS):
        around = turn(u, 1) + turn(u, -1)
        if before is not None:
            around = around + before
        if s + 1 < ROWS:
            after, conduct_after = load(s + 1), k_ref[s + 1 : s + 2, :]
            u_after = after * conduct_after
            around = around + u_after
        store(s, (1.0 - 4.0 * conduct * conduct) * here + conduct * around)
        if s + 1 < ROWS:
            before, here, conduct, u = u, after, conduct_after, u_after


def piece(value, q):
    return value[:, q * LANES : (q + 1) * LANES]


def moved(take, source, target, lane):
    a, first = source // LANES, source % LANES
    cells = take(a)
    if first + TC > LANES:
        cells = jnp.where(lane >= first, cells, take(a + 1))
    return turn(cells, target - source)


def spread_body(x_ref, out_ref, kept_ref, code_ref, z_ref, w_ref, table_ref, slot_ref, sem):
    lane = lanes_of((8, LANES))
    z_ref[0:2048, :] = x_ref[...].astype(F32)
    codes = z_ref[pl.ds(PIECES - 1, ROWS, stride=64), :]
    line = lanes_of((ROWS, LANES))
    codes = jnp.where(line < NB, turn(codes, -IDX - NB) * ROWS + turn(codes, -IDX), 0.0)
    code_ref[...] = jnp.transpose(codes)[0:NB, :].astype(jnp.int32)
    slot_copy = pltpu.make_async_copy(code_ref, slot_ref, sem)
    slot_copy.start()
    for q in range(PIECES):
        hi, lo = q, PIECES + q
        kept_ref[:, q * LANES : (q + 1) * LANES] = (
            z_ref[pl.ds((hi // 2) * 8 + 6 + hi % 2, ROWS, stride=64), :]
            + z_ref[pl.ds((lo // 2) * 8 + 6 + lo % 2, ROWS, stride=64), :]
        )

    def arrived(s):
        return jnp.concatenate([z_ref[pl.ds(s * 64 + q, 8, stride=8), :] for q in range(PIECES)], axis=1)

    def keep(s, value):
        w_ref[s] = value

    def cut(s, value):
        for c in range(COLS):
            table_ref[c * ROWS + s] = moved(lambda a: piece(value, a), c * TC, 0, lane)

    sweep(arrived, kept_ref, keep)
    sweep(lambda s: w_ref[s], kept_ref, keep)
    for s in range(ROWS):
        cut(s, w_ref[s])
    table_ref[BLANK] = jnp.zeros((8, LANES), F32)

    slot_copy.wait()
    ahead = 2
    waiting = {}
    for s in range(ROWS + ahead):
        if s < ROWS:
            waiting[s] = [table_ref[slot_ref[j, s]] for j in range(NB)]
        if s >= ahead:
            tiles = waiting.pop(s - ahead)
            runs = [[], [], []]
            for j in range(NB):
                for _, b, low, high, rotation in span(j * TC, 0):
                    runs[b].append((low, high, turn(tiles[j], rotation)))
            for b in range(3):
                out_ref[s - ahead, :, b * LANES : (b + 1) * LANES] = chain(runs[b], lane).astype(BF16)


def observe_body(x_ref, f_ref, weight_ref, out_ref, x2_ref, g_ref):
    lane = lanes_of((8, LANES))
    runs = {}
    for tau in range(TW):
        value = x_ref[tau].astype(F32)
        for j in range(NB):
            cells = moved(lambda a: piece(value, a), j * TC, tau * TC, lane)
            for _, b, low, high, _ in span(tau * TC, 0):
                runs.setdefault((j, b), []).append((low, high, cells))
        for key in [key for key in runs if (key[1] + 1) * LANES <= (tau + 1) * TC or tau == TW - 1]:
            j, b = key
            x2_ref[j, :, b * LANES : (b + 1) * LANES] = chain(runs.pop(key), lane)
    total = jnp.zeros((8, 64), F32)
    for j in range(NB):
        total = total + lax.dot_general(
            x2_ref[j, :, 0 : TW * TC].astype(BF16),
            f_ref[j],
            (((1,), (1,)), ((), ())),
            preferred_element_type=F32,
        )
    weighted = (weight_ref[...] * total).astype(BF16)
    for j in range(NB):
        g_ref[j, :, 0 : TW * TC] = jnp.dot(weighted, f_ref[j], preferred_element_type=F32)
    for tau in range(TW):
        runs = [[], [], []]
        for j in range(NB):
            cells = moved(lambda a: g_ref[j, :, a * LANES : (a + 1) * LANES], tau * TC, j * TC, lane)
            for _, b, low, high, _ in span(j * TC, 0):
                runs[b].append((low, high, cells))
        for b in range(3):
            out_ref[tau, :, b * LANES : (b + 1) * LANES] = chain(runs[b], lane).astype(BF16)
    out_ref[TW:TWP] = jnp.zeros((TWP - TW, 8, NB * TC), BF16)


def collect_body(slot_any, x_ref, k_ref, out_ref, z_ref, w_ref, table_ref, pieces_ref, slot_ref, sem):
    slot_copy = pltpu.make_async_copy(slot_any, slot_ref, sem)
    slot_copy.start()
    lane = lanes_of((8, LANES))
    table_ref[...] = jnp.zeros(table_ref.shape, F32)
    for s in range(ROWS):
        value = x_ref[s].astype(F32)
        for j in range(NB):
            pieces_ref[s * NB + j] = moved(lambda a: piece(value, a), j * TC, 0, lane)
    slot_copy.wait()

    def reader(s, carry):
        tiles = [slot_ref[j, s] for j in range(NB)]
        sums = []
        for j in range(NB):
            sums.append(table_ref[tiles[j]] + pieces_ref[s * NB + j])
        for j in range(NB):
            table_ref[tiles[j]] = sums[j]
        return carry

    lax.fori_loop(0, ROWS, reader, 0, unroll=True)

    def joined(s):
        runs = [[] for _ in range(PIECES)]
        for c in range(COLS):
            tile = table_ref[c * ROWS + s]
            for _, b, low, high, rotation in span(c * TC, 0):
                runs[b].append((low, high, turn(tile, rotation)))
        runs[-1].append((TAIL, TAIL + 2, turn(table_ref[s], TAIL)))
        runs[-1].append((TAIL + 2, LANES - 2, jnp.zeros((8, LANES), F32)))
        runs[-1].append((LANES - 2, LANES, turn(table_ref[(COLS - 1) * ROWS + s], TAIL)))
        return jnp.concatenate([chain(run, lane) for run in runs], axis=1)

    def keep(s, value):
        w_ref[s] = value

    def leave(s, value):
        for q in range(PIECES):
            z_ref[pl.ds(s * 8 * PIECES + q, 8, stride=PIECES), :] = piece(value, q)

    for s in range(ROWS):
        keep(s, joined(s))
    for _ in range(DIFF):
        sweep(lambda s: w_ref[s], k_ref, keep)
    for s in range(ROWS):
        leave(s, w_ref[s])
    out_ref[...] = z_ref[0:1536, :].astype(BF16)


def unmix_body(x_ref, hi_ref, lo_ref, out_ref, z_ref, w_ref):
    z_ref[0:1536, :] = x_ref[...].astype(F32)
    for w in range(NW):
        for q in range(PIECES):
            w_ref[TWP * w : TWP * (w + 1), q * LANES : (q + 1) * LANES] = z_ref[
                pl.ds(w * PIECES + q, TWP, stride=NW * PIECES), :
            ].astype(BF16)
    x = w_ref[...]
    down = (((0,), (0,)), ((), ()))
    mixed = lax.dot_general(hi_ref[...], x, down, preferred_element_type=F32) + lax.dot_general(
        lo_ref[...], x, down, preferred_element_type=F32
    )
    out_ref[...] = mixed.astype(BF16)


def image_body(x_ref, d_ref, r_ref, image_ref, sums_ref, z_ref):
    for q in range(PIECES):
        z_ref[q, 0:256, :] = x_ref[:, q * LANES : (q + 1) * LANES].astype(F32)
    totals = [jnp.zeros((8, 1), F32) for _ in range(4)]
    for q in range(PIECES):
        width = TAIL if q == PIECES - 1 else LANES
        at = pl.ds(q * LANES, width)
        sums = [jnp.zeros((8, width), F32) for _ in range(4)]
        for t in range(TW):
            d = d_ref[t, :, at]
            r = r_ref[t, :, at]
            image = d + z_ref.at[q][pl.ds(t, 8, stride=TWP), :][:, 0:width]
            image_ref[t, :, at] = image
            for i, (left, right) in enumerate(((r, r), (d, image), (r, image), (image, image))):
                sums[i] = sums[i] + left * right
        for i in range(4):
            totals[i] = totals[i] + jnp.sum(sums[i], axis=1, keepdims=True)
    lane = lanes_of((8, LANES))
    k = lax.broadcasted_iota(jnp.int32, (8, LANES), 0)
    spread = jnp.zeros((8, LANES), F32)
    for i in range(4):
        spread = jnp.where(lane == k * 4 + i, totals[i], spread)
    line = jnp.sum(spread, axis=0, keepdims=True)
    sums_ref[...] = jnp.broadcast_to(line, sums_ref.shape)


def update_body(sums_ref, it_ref, r_ref, d_ref, image_ref, it_out, r_out, d_out, it_new, r_new, d_new, sem):
    line = jnp.sum(sums_ref[...], axis=0, keepdims=True)
    lane = lanes_of((8, LANES))
    k = lax.broadcasted_iota(jnp.int32, (8, LANES), 0)
    rr, dq, rq, qq = [
        jnp.sum(jnp.where(lane == k * 4 + i, line, 0.0), axis=1, keepdims=True) for i in range(4)
    ]
    step = rr / dq
    norm = jnp.maximum(rr + step * (step * qq - 2.0 * rq), 0.0)
    ratio = norm / rr
    copies = []
    for i, (start, stop) in enumerate(((0, 3), (3, 12), (12, 21), (21, TW))):
        for t in range(start, stop):
            d = d_ref[t]
            after = r_ref[t] - step * image_ref[t]
            it_new[t] = it_ref[t] + step * d
            r_new[t] = after
            d_new[t] = after + ratio * d
        at = pl.ds(start, stop - start)
        for n, (new, out) in enumerate(((it_new, it_out), (r_new, r_out), (d_new, d_out))):
            copies.append(pltpu.make_async_copy(new.at[at], out.at[at], sem.at[n, i]))
            copies[-1].start()
    for copy in copies:
        copy.wait()


def shape(dims, dtype):
    return jax.ShapeDtypeStruct(dims, dtype)


def local(
    iterate, residual, direction, diffusivity, temporal_factor, block_tile, footprints, obs_weight
):
    both = ("space", "tm")
    iterate, residual, direction = [
        jnp.transpose(value, (1, 0, 2)) for value in (iterate, residual, direction)
    ]
    grid = (ROWS, 8, WIDE)
    with jax.named_scope("prepare"):
        message, hi, lo, cut = call(
            prepare_body,
            (
                shape((8, TWP, WIDE), BF16),
                shape((256, 256), BF16),
                shape((256, 256), BF16),
                shape((16, LANES), F32),
            ),
            [
                pltpu.VMEM((PIECES, 264, LANES), F32),
                pltpu.VMEM((240, TAIL), F32),
                pltpu.VMEM((240, LANES), F32),
                pltpu.SMEM((1, NB), jnp.int32),
                pltpu.VMEM((240, 240), F32),
                pltpu.VMEM((240, 256), F32),
                pltpu.VMEM((256, 256), F32),
                pltpu.VMEM((LON,), F32),
                pltpu.VMEM((8, LANES), F32),
                pltpu.SemaphoreType.DMA((6,)),
                pltpu.SemaphoreType.DMA((3,)),
            ],
            "hhhh",
        )(
            *[
                pltpu.with_memory_space_constraint(value, pltpu.HBM)
                for value in (block_tile, direction.reshape(240, LON), temporal_factor, diffusivity)
            ]
        )
        message = lax.all_to_all(message, "tm", 0, 0, tiled=True)
    with jax.named_scope("mix"):
        message = call(mix_body, shape((2048, LANES), BF16), [pltpu.VMEM((2112, LANES), F32)])(
            message.reshape(256, WIDE), hi, lo, cut
        )
        message = lax.all_to_all(message.reshape(256, 8, LANES), both, 0, 0, tiled=True)
    with jax.named_scope("spread"):
        message, conduct, slots = call(
            spread_body,
            (shape((ROWS, 8, NB * TC), BF16), shape((ROWS, WIDE), F32), shape((NB, ROWS), jnp.int32)),
            [
                pltpu.VMEM((2112, LANES), F32),
                pltpu.VMEM(grid, F32),
                pltpu.VMEM((BLANK + 1, 8, LANES), F32),
                pltpu.SMEM((NB, ROWS), jnp.int32),
                pltpu.SemaphoreType.DMA,
            ],
        )(message.reshape(2048, LANES))
        message = lax.all_to_all(message, "space", 0, 0, tiled=True)
    with jax.named_scope("observe"):
        message = call(
            observe_body,
            shape((TWP, 8, NB * TC), BF16),
            [pltpu.VMEM((NB, 8, 1536), F32), pltpu.VMEM((NB, 8, 1536), F32)],
        )(message, footprints[0], obs_weight[0])
        message = lax.all_to_all(message, "space", 0, 0, tiled=True)
    with jax.named_scope("collect"):
        message = call(
            collect_body,
            shape((1536, LANES), BF16),
            [
                pltpu.VMEM((1584, LANES), F32),
                pltpu.VMEM(grid, F32),
                pltpu.VMEM((BLANK + 1, 8, LANES), F32),
                pltpu.VMEM((ROWS * NB, 8, LANES), F32),
                pltpu.SMEM((NB, ROWS), jnp.int32),
                pltpu.SemaphoreType.DMA,
            ],
            "h",
        )(slots, message, conduct)
        message = lax.all_to_all(message.reshape(768, 2, LANES), both, 0, 0, tiled=True)
    with jax.named_scope("unmix"):
        message = call(
            unmix_body,
            shape((256, WIDE), BF16),
            [pltpu.VMEM((1584, LANES), F32), pltpu.VMEM((256, WIDE), BF16)],
        )(message.reshape(1536, LANES), hi, lo)
        message = lax.all_to_all(message.reshape(8, TWP, WIDE), "tm", 0, 0, tiled=True)
    with jax.named_scope("image"):
        image, sums = call(
            image_body,
            (shape((TW, 8, LON), F32), shape((256, LANES), F32)),
            [pltpu.VMEM((PIECES, 288, LANES), F32)],
        )(message.reshape(256, WIDE), direction, residual)
        sums = lax.all_to_all(sums, both, 0, 0, tiled=True)
    with jax.named_scope("update"):
        whole = (TW, 8, LON)
        outs = call(
            update_body,
            tuple(shape(whole, F32) for _ in range(3)),
            [pltpu.VMEM(whole, F32) for _ in range(3)] + [pltpu.SemaphoreType.DMA((3, 4))],
            out_places="hhh",
        )(sums, iterate, residual, direction, image)
    return tuple(jnp.transpose(value, (1, 0, 2)) for value in outs)


def solution(mesh):
    return jax.shard_map(
        local,
        mesh=mesh,
        in_specs=(
            P(None, "tm", "space"),
            P(None, "tm", "space"),
            P(None, "tm", "space"),
            P("space"),
            P(),
            P("tm", "space"),
            P("tm", "space", None, None),
            P("tm", "space", None),
        ),
        out_specs=(P(None, "tm", "space"), P(None, "tm", "space"), P(None, "tm", "space")),
        check_vma=False,
    )
```
